128 devices in a mesh: dst: 32 (over x, y, core), src: 4 (over z).
Axes of the slice: x: 4, y: 4, z: 4, core: 2. Of those that a mesh axis runs over, the one named last changes fastest.
Arguments:
- features: bfloat16 [32768, 512], P(('dst', 'src'))
- w_query: bfloat16 [512, 512], replicated
- w_key: bfloat16 [512, 512], replicated
- w_value: bfloat16 [512, 512], replicated, may hold values from -0.25 to 0.25
- w_out: bfloat16 [512, 512], replicated, may hold values from -0.25 to 0.25
- node_bits: int32 [32768], P('dst'), may hold values from 0 to 1073741823
- block_src: int32 [256, 4, 32], P('dst', 'src'), may hold values from 0 to 63, as said below
- block_count: int32 [256, 4], P('dst', 'src'), may hold values from 0 to 32, as said below
- graph_ids: int32 [32768], P(('dst', 'src')), may hold values from 0 to 3, as said below
Outputs:
- updated: bfloat16 [32768, 512], P(('dst', 'src'))
- pooled: float32 [4, 512], replicated
The draws below stay inside these ranges and needn't reach their ends.
Inputs may be any that keep to these rules, and one draw needn't show every extreme that they name: For destination block b and group s only the first block_count[b, s] entries of block_src[b, s] are used; they are distinct blocks of the group, all in the graph of block b. The group that holds block b itself lists that block first. `block_count`: the group that holds a destination block lists 1 or more blocks for it. `graph_ids`: graph ids never fall along the nodes; every graph holds one or more whole blocks of 128 nodes.
All inputs are finite; a program needn't handle non-finite values.
Results may differ from the reference program's by a relative error of at most 0.0078.
Values may be sent and summed in bfloat16 or wider, within the bound.
A program may use at most 128 MiB of HBM per device.

```python
import math
import jax
import jax.numpy as jnp
from jax import lax

D = 512
HEADS = 8
BLK = 128
GRAPHS = 4
NPD = 256
NODES = 32768
NBLK = 256
KMAX = 32
N_DST = 32
N_SRC = 4


def draw_features(key, part):
    return jnp.clip(jax.random.normal(jax.random.fold_in(key, 13), (NODES, D), jnp.float32), -6.0, 6.0).astype(jnp.bfloat16)


def query_key_pair(key):
    spread = 1.6 / math.sqrt(D)
    first_draw = jnp.clip(jax.random.normal(jax.random.fold_in(key, 21), (D, D), jnp.float32), -6.0, 6.0) * spread
    other_draw = jnp.clip(jax.random.normal(jax.random.fold_in(key, 22), (D, D), jnp.float32), -6.0, 6.0) * spread
    return (first_draw, other_draw)


def draw_w_query(key, part):
    return query_key_pair(key)[0].astype(jnp.bfloat16)


def draw_w_key(key, part):
    return query_key_pair(key)[1].astype(jnp.bfloat16)


def graph_layout(key):
    blocks = jnp.arange(NBLK, dtype=jnp.int32)
    large_length = NBLK // 2 + jax.random.randint(jax.random.fold_in(key, 41), (), NBLK // 8, NBLK // 4, dtype=jnp.int32)
    remaining = NBLK - large_length
    first_small = jax.random.randint(jax.random.fold_in(key, 42), (), 1, remaining // 3 + 1, dtype=jnp.int32)
    second_small = jax.random.randint(jax.random.fold_in(key, 43), (), 1, remaining // 3 + 1, dtype=jnp.int32)
    edge_one = large_length
    edge_two = large_length + first_small
    edge_three = edge_two + second_small
    flipped = jax.random.randint(jax.random.fold_in(key, 44), (), 0, 2, dtype=jnp.int32)
    mirrored = jnp.where(flipped == 1, NBLK - 1 - blocks, blocks)
    drawn_ids = (mirrored >= edge_one).astype(jnp.int32) + (mirrored >= edge_two).astype(jnp.int32) + (mirrored >= edge_three).astype(jnp.int32)
    block_graph = jnp.where(flipped == 1, GRAPHS - 1 - drawn_ids, drawn_ids).astype(jnp.int32)
    large_first = jnp.where(flipped == 1, NBLK - large_length, 0).astype(jnp.int32)
    return (block_graph, large_first)


def draw_graph_ids(key, part):
    block_graph = graph_layout(key)[0]
    return jnp.repeat(block_graph, BLK).astype(jnp.int32)


def block_lists(key):
    per_shard = NPD // BLK
    groups = N_DST * NPD // BLK
    block_graph, large_first = graph_layout(key)
    blocks = jnp.arange(NBLK, dtype=jnp.int32)
    shard = blocks // per_shard
    own_src = shard % N_SRC
    own_group = shard // N_SRC * per_shard + blocks % per_shard
    group_ids = jnp.arange(N_SRC, dtype=jnp.int32)
    group_range = jnp.arange(groups, dtype=jnp.int32)
    global_block = (group_range[None, :] // per_shard * N_SRC + group_ids[:, None]) * per_shard + group_range[None, :] % per_shard
    candidate = block_graph[global_block][None, :, :] == block_graph[:, None, None]
    candidate_count = jnp.sum(candidate.astype(jnp.int32), axis=-1)
    levels = jnp.left_shift(jnp.int32(1), jax.random.randint(jax.random.fold_in(key, 31), (N_DST,), 0, 4, dtype=jnp.int32))
    block_level = levels[blocks // (N_SRC * per_shard)]
    upper = KMAX * block_level // 8 + 1
    lower = KMAX * (block_level - 1) // 16
    counts = jax.random.randint(jax.random.fold_in(key, 32), (NBLK, N_SRC), lower[:, None], upper[:, None], dtype=jnp.int32)
    self_column = own_src[:, None] == group_ids[None, :]
    counts = jnp.where(self_column, jnp.maximum(counts, 1), counts)
    counts = jnp.minimum(counts, candidate_count)
    forced_group = jax.random.randint(jax.random.fold_in(key, 34), (), 0, N_SRC, dtype=jnp.int32)
    counts = jnp.where((blocks[:, None] == large_first) & (group_ids[None, :] == forced_group), KMAX, counts)
    ranking = jax.random.randint(jax.random.fold_in(key, 35), (NBLK, N_SRC, groups), 0, 1048576, dtype=jnp.int32) * groups + group_range
    ranking = jnp.where(candidate, ranking, ranking + 536870912)
    ranking = jnp.where(self_column[:, :, None] & (group_range[None, None, :] == own_group[:, None, None]), -1, ranking)
    order = jnp.argsort(ranking, axis=-1)[:, :, :KMAX].astype(jnp.int32)
    return (order, counts.astype(jnp.int32))


def draw_block_src(key, part):
    return block_lists(key)[0]


def draw_block_count(key, part):
    return block_lists(key)[1]


def place_ends(array, rng, low, high):
    longest = array.shape.index(max(array.shape))
    spots = []
    for shift in (0, 1):
        where = [jax.random.randint(jax.random.fold_in(rng, axis), (), 0, length) for axis, length in enumerate(array.shape)]
        where[longest] = (where[longest] + shift) % array.shape[longest]
        spots.append(tuple(where))
    return array.at[spots[0]].set(low).at[spots[1]].set(high)


def noise(stream_key, dims, scale, most, kind=jnp.bfloat16):
    result = scale * jax.random.normal(stream_key, dims, jnp.float32)
    return jnp.clip(result, min=-most, max=most).astype(kind)


def setup_inputs(seed: int = 0) -> dict:
    seeds = jax.random.split(jax.random.key(seed), 10)
    features = draw_features(jax.random.fold_in(seeds[9], 71), 0)
    w_query = draw_w_query(jax.random.fold_in(seeds[9], 71), 0)
    w_key = draw_w_key(jax.random.fold_in(seeds[9], 71), 0)
    w_value = noise(seeds[3], (D, D), D ** -0.5, 0.25)
    w_out = noise(seeds[4], (D, D), D ** -0.5, 0.25)
    node_bits = place_ends(jax.random.randint(seeds[5], (NODES,), 0, 1073741824), jax.random.fold_in(seeds[5], 1), 0, 1073741823).astype(jnp.int32)
    block_src = draw_block_src(jax.random.fold_in(seeds[9], 71), 0)
    block_count = draw_block_count(jax.random.fold_in(seeds[9], 71), 0)
    graph_ids = draw_graph_ids(jax.random.fold_in(seeds[9], 71), 0)
    return dict(features=features, w_query=w_query, w_key=w_key, w_value=w_value, w_out=w_out, node_bits=node_bits, block_src=block_src, block_count=block_count, graph_ids=graph_ids)


NEG_FLOOR = -1e+30

def reference(features, w_query, w_key, w_value, w_out, node_bits, block_src, block_count, graph_ids):
    node_total, model_width = features.shape
    head_depth = model_width // HEADS
    per_shard = NPD // BLK
    block_total = node_total // BLK

    def project(weight):
        return jnp.dot(features, weight, preferred_element_type=jnp.float32).astype(jnp.bfloat16)
    query_tiles = project(w_query).reshape(block_total, BLK, HEADS, head_depth)
    key_tiles = project(w_key).reshape(block_total, BLK, HEADS, head_depth)
    value_tiles = project(w_value).reshape(block_total, BLK, HEADS, head_depth)
    bit_tiles = node_bits.reshape(block_total, BLK)
    lane_ids = jnp.arange(BLK, dtype=jnp.int32)
    group_ids = jnp.arange(N_SRC, dtype=jnp.int32)
    slot_ids = jnp.arange(KMAX, dtype=jnp.int32)

    def one_block(block_place):
        slot_rows = block_src[block_place]
        slot_total = block_count[block_place]
        live_slot = slot_ids[None, :] < slot_total[:, None]
        starts = (slot_rows // per_shard * N_SRC + group_ids[:, None]) * NPD + slot_rows % per_shard * BLK
        source_blocks = (starts // BLK).reshape(-1)
        key_part = key_tiles[source_blocks].reshape(-1, HEADS, head_depth).astype(jnp.float32)
        value_part = value_tiles[source_blocks].reshape(-1, HEADS, head_depth).astype(jnp.float32)
        src_ids = (starts.reshape(-1, 1) + lane_ids[None, :]).reshape(-1)
        dst_ids = block_place * BLK + lane_ids
        bit_on = jnp.right_shift(bit_tiles[block_place][:, None], (src_ids % 30)[None, :]) & 1
        edge_mask = ((bit_on == 1) | (dst_ids[:, None] == src_ids[None, :])) & jnp.repeat(live_slot.reshape(-1), BLK)[None, :]
        scores = jnp.einsum('qhd,khd->qhk', query_tiles[block_place].astype(jnp.float32), key_part) * (1.0 / math.sqrt(head_depth))
        masked = jnp.where(edge_mask[:, None, :], scores, NEG_FLOOR)
        highest = lax.optimization_barrier(jnp.max(masked, axis=-1, keepdims=True))
        weights = jnp.where(edge_mask[:, None, :], jnp.exp(masked - highest), 0.0)
        denominator = lax.optimization_barrier(jnp.sum(weights, axis=-1))
        rounded = lax.optimization_barrier(weights.astype(jnp.bfloat16)).astype(jnp.float32)
        numerator = jnp.einsum('qhk,khd->qhd', rounded, value_part)
        return (numerator / denominator[:, :, None]).astype(jnp.bfloat16).reshape(BLK, model_width)
    attention = lax.map(one_block, jnp.arange(block_total, dtype=jnp.int32)).reshape(node_total, model_width)
    mixed = jnp.dot(attention, w_out, preferred_element_type=jnp.float32)
    updated = (features.astype(jnp.float32) + mixed).astype(jnp.bfloat16)
    graph_sums = jax.ops.segment_sum(updated.astype(jnp.float32), graph_ids, num_segments=GRAPHS)
    node_counts = jax.ops.segment_sum(jnp.ones((node_total,), jnp.float32), graph_ids, num_segments=GRAPHS)
    pooled = graph_sums / jnp.sqrt(node_counts)[:, None]
    return (updated, pooled)
```

```python
import functools

import jax
import jax.numpy as jnp
from jax import lax
from jax.experimental import pallas as pl
from jax.experimental.pallas import tpu as pltpu
from jax.sharding import PartitionSpec as P

MESH = pl.DeviceIdType.MESH
BF, F32, I32 = jnp.bfloat16, jnp.float32, jnp.int32
WIDTH, HEADS, HD, BLK, ROWS = 512, 8, 64, 128, 256
SLOTS = 32
OUT_MASK = -3e38
FLOOR = -1e30
RING = 4
NBUF = 4


def place():
    d = lax.axis_index("dst")
    return d // 8, (d // 2) % 4, d % 2, lax.axis_index("src")


def dst_index(x, y, core):
    return (x % 4) * 8 + (y % 4) * 2 + core


def flip(a, b):
    return a + b - 2 * a * b


def nt(a, b):
    return lax.dot_general(a, b, (((1,), (1,)), ((), ())), preferred_element_type=F32)


def gather_kernel(
    feat, wq, wk, wv, ints,
    kb, vt, q_out, ints_out, dq_out, self_score, self_value,
    fbuf, kk, vv, wqt, wkt, wvt, dq, got,
    ring_send, ring_recv, sib_send, sib_recv, z_send, z_recv, i_send, i_recv, out_sem,
):
    x, y, c, z = place()
    me = dst_index(x, y, c)
    sibling = dst_index(x, y, 1 - c)

    def blk(core, i, j):
        return dst_index(x + (1 - core) * i + core * j, y + core * i + (1 - core) * j, core)

    zup, zdown = (z + 1) % 4, (z + 3) % 4
    peers = [(dst_index(x + 1, y, c), z), (dst_index(x + 3, y, c), z), (me, zup), (me, zdown)]
    for dy in range(4):
        for dc in range(2):
            if dy or dc:
                peers.append((dst_index(x, y + dy, flip(c, dc)), z))
    fbuf[me] = feat[...]
    barrier = pltpu.get_barrier_semaphore()
    for peer in peers:
        pl.semaphore_signal(barrier, inc=1, device_id=peer, device_id_type=MESH)
    pl.semaphore_wait(barrier, len(peers))

    def remote(src, dst, send, recv, to):
        return pltpu.make_async_remote_copy(
            src_ref=src, dst_ref=dst, send_sem=send, recv_sem=recv, device_id=to, device_id_type=MESH
        )

    sent = []

    def go(copy):
        copy.start()
        sent.append(copy)

    def along(row, step):
        if row == 0:
            return (blk(c, step, 0), z)
        return (blk(c, 0, step), z)

    def full(row, i, step):
        b = blk(c, i, 0)
        s = 0 if step == 1 else 1
        go(remote(fbuf.at[b], fbuf.at[b], ring_send.at[row, s], ring_recv.at[row, s], along(row, step)))

    def fulls(row, i):
        full(row, i, 1)
        full(row, i, 3)

    def half_ref(row, i, at, part):
        b = blk(c, at, 0) if row == 0 else blk(c, i, at)
        return fbuf.at[b, pl.ds(part * BLK, BLK)]

    def forward(row, i):
        for part, frm, step in ((0, 3, 1), (1, 1, 3)):
            r = half_ref(row, i, frm, part)
            go(remote(r, r, ring_send.at[row, 2 + part], ring_recv.at[row, 2 + part], along(row, step)))

    def wait_full(row, i):
        for s, frm in ((0, 3), (1, 1)):
            b = blk(c, frm, 0) if row == 0 else blk(c, i, frm)
            remote(fbuf.at[b], fbuf.at[b], ring_send.at[row, s], ring_recv.at[row, s], (sibling, z)).wait_recv()

    def wait_half(row, i):
        for part in range(2):
            r = half_ref(row, i, 2, part)
            remote(r, r, ring_send.at[row, 2 + part], ring_recv.at[row, 2 + part], (sibling, z)).wait_recv()

    def share(i, j):
        b = blk(c, i, j)
        go(remote(fbuf.at[b], fbuf.at[b], sib_send.at[i, j], sib_recv.at[i, j], (sibling, z)))

    def wait_share(i, j):
        b = blk(1 - c, i, j)
        remote(fbuf.at[b], fbuf.at[b], sib_send.at[i, j], sib_recv.at[i, j], (sibling, z)).wait_recv()

    def store(b, n):
        return [
            pltpu.make_async_copy(kk.at[b], kb.at[b], out_sem.at[b, 0]),
            pltpu.make_async_copy(vv.at[b], vt.at[b], out_sem.at[b, 1]),
        ]

    def project(b):
        f = fbuf[b]
        kk[b] = jnp.dot(f, wk[...], preferred_element_type=F32).astype(BF)
        v = nt(wvt[...], f).astype(BF)
        vv[b, 0] = v[:, :BLK]
        vv[b, 1] = v[:, BLK:]
        for copy in store(b, 0):
            copy.start()

    def project_many(n, where):
        def body(e, carry):
            project(where(e))
            return carry

        lax.fori_loop(0, n, body, 0)

    fulls(0, 0)
    fulls(1, 0)
    share(0, 0)
    for dy in range(4):
        for dc in range(2):
            s = (2 * y + dy) % 4
            src = ints.at[2 * s + dc]
            slot = 2 * s + c
            if dy == 0 and dc == 0:
                local_ints = pltpu.make_async_copy(src, got.at[slot], i_recv.at[dy, dc])
                local_ints.start()
            else:
                go(
                    remote(
                        src, got.at[slot], i_send.at[dy, dc], i_recv.at[dy, dc],
                        (dst_index(x, y + dy, flip(c, dc)), z),
                    )
                )
    wvt[...] = wv[...].T
    wqt[...] = wq[...].T
    wkt[...] = wk[...].T
    project(me)

    wait_full(0, 0)
    forward(0, 0)
    fulls(4, 3)
    fulls(2, 1)
    share(3, 0)
    share(1, 0)
    wait_full(1, 0)
    forward(1, 0)
    share(0, 3)
    share(0, 1)
    project_many(4, lambda e: blk(c, (1 - e // 2) * (1 + 2 * e), (e // 2) * (2 * e - 3)))
    wait_share(0, 0)
    project(sibling)

    wait_half(0, 0)
    fulls(3, 2)
    share(2, 0)
    wait_half(1, 0)
    share(0, 2)
    project_many(2, lambda e: blk(c, 2 - 2 * e, 2 * e))
    for i, j in ((1, 0), (3, 0), (0, 1), (0, 3)):
        wait_share(i, j)
    project_many(4, lambda e: blk(1 - c, (1 - e // 2) * (1 + 2 * e), (e // 2) * (2 * e - 3)))
    wait_share(2, 0)
    wait_share(0, 2)

    yy = (z - y + 4) % 4

    def plane_rows(cc):
        return fbuf.at[dst_index(x, yy, cc), pl.ds(pl.multiple_of(flip(c, cc) * BLK, BLK), BLK)]

    for up, to in ((0, zup), (1, zdown)):
        for cc in range(2):
            go(remote(plane_rows(cc), dq.at[z, cc], z_send.at[up, cc], z_recv.at[up, cc], (me, to)))
    own_copies = [pltpu.make_async_copy(plane_rows(cc), dq.at[z, cc], z_recv.at[3, cc]) for cc in range(2)]
    for copy in own_copies:
        copy.start()

    wait_full(4, 3)
    forward(4, 3)
    share(3, 3)
    share(3, 1)
    wait_full(2, 1)
    forward(2, 1)
    share(1, 3)
    share(1, 1)
    project_many(4, lambda e: blk(c, 1 + 2 * (e // 2), 1 + 2 * (e % 2)))
    project_many(2, lambda e: blk(1 - c, 2 - 2 * e, 2 * e))

    wait_half(4, 3)
    share(3, 2)
    wait_half(2, 1)
    share(1, 2)
    for up, frm in ((0, zdown), (1, zup)):
        for cc in range(2):
            remote(dq.at[frm, cc], dq.at[frm, cc], z_send.at[up, cc], z_recv.at[up, cc], (me, zup)).wait_recv()
    for cc, frm, to in ((0, zdown, zup), (1, zup, zdown)):
        go(remote(dq.at[frm, cc], dq.at[frm, cc], z_send.at[2, cc], z_recv.at[2, cc], (me, to)))
    project_many(2, lambda e: blk(c, 1 + 2 * e, 2))
    for i in (1, 3):
        for j in (1, 3):
            wait_share(i, j)
    project_many(4, lambda e: blk(1 - c, 1 + 2 * (e // 2), 1 + 2 * (e % 2)))

    wait_full(3, 2)
    forward(3, 2)
    share(2, 3)
    share(2, 1)
    project_many(2, lambda e: blk(c, 2, 1 + 2 * e))
    wait_share(1, 2)
    wait_share(3, 2)
    project_many(2, lambda e: blk(1 - c, 1 + 2 * e, 2))
    for copy in own_copies:
        copy.wait()

    def query(s, cc):
        q = nt(wqt[...], dq[s, cc]).astype(BF)
        q_out[2 * s + cc] = q * 0.125

    def queries(e, carry):
        query((z + 3 + e // 2) % 4, e % 2)
        return carry

    lax.fori_loop(0, 6, queries, 0)
    for cc in range(2):
        f = dq[z, cc]
        dq_out[cc] = f
        k = nt(wkt[...], f).astype(BF).astype(F32)
        q = q_out[2 * z + cc].astype(F32)
        prod = k * q
        self_score[cc] = jnp.concatenate(
            [jnp.sum(prod[h * HD : (h + 1) * HD], axis=0, keepdims=True) for h in range(HEADS)], axis=0
        )
        self_value[cc] = nt(wvt[...], f).astype(BF)
    local_ints.wait()
    for dy in range(4):
        for dc in range(2):
            if dy or dc:
                slot = 2 * ((2 * y + 4 - dy) % 4) + flip(c, dc)
                remote(
                    got.at[slot], got.at[slot], i_send.at[dy, dc], i_recv.at[dy, dc], (sibling, z)
                ).wait_recv()
    ints_out[...] = got[...]

    wait_half(3, 2)
    share(2, 2)
    project(blk(c, 2, 2))
    wait_share(2, 1)
    wait_share(2, 3)
    project_many(2, lambda e: blk(1 - c, 2, 1 + 2 * e))
    far = (z + 2) % 4
    for cc in range(2):
        remote(dq.at[far, cc], dq.at[far, cc], z_send.at[2, cc], z_recv.at[2, cc], (me, zup)).wait_recv()
    for cc in range(2):
        query(far, cc)
    wait_share(2, 2)
    project(blk(1 - c, 2, 2))

    def drain(b, carry):
        for copy in store(b, 0):
            copy.wait()
        return carry

    lax.fori_loop(0, 32, drain, 0)
    for copy in sent:
        copy.wait_send()


def gather_call(feat, wq, wk, wv, ints):
    vm = pl.BlockSpec(memory_space=pltpu.VMEM)
    anyw = pl.BlockSpec(memory_space=pl.ANY)
    dma = pltpu.SemaphoreType.DMA
    return pl.pallas_call(
        gather_kernel,
        out_shape=(
            jax.ShapeDtypeStruct((32, ROWS, WIDTH), BF),
            jax.ShapeDtypeStruct((32, 2, WIDTH, BLK), BF),
            jax.ShapeDtypeStruct((8, WIDTH, BLK), BF),
            jax.ShapeDtypeStruct((8, 8, BLK), I32),
            jax.ShapeDtypeStruct((2, BLK, WIDTH), BF),
            jax.ShapeDtypeStruct((2, HEADS, BLK), F32),
            jax.ShapeDtypeStruct((2, WIDTH, BLK), BF),
        ),
        in_specs=[vm] * 5,
        out_specs=(anyw, anyw, vm, vm, vm, vm, vm),
        scratch_shapes=[
            pltpu.VMEM((32, ROWS, WIDTH), BF),
            pltpu.VMEM((32, ROWS, WIDTH), BF),
            pltpu.VMEM((32, 2, WIDTH, BLK), BF),
            pltpu.VMEM((WIDTH, WIDTH), BF),
            pltpu.VMEM((WIDTH, WIDTH), BF),
            pltpu.VMEM((WIDTH, WIDTH), BF),
            pltpu.VMEM((4, 2, BLK, WIDTH), BF),
            pltpu.VMEM((8, 8, BLK), I32),
            dma((5, 4)), dma((5, 4)), dma((4, 4)), dma((4, 4)),
            dma((3, 2)), dma((4, 2)), dma((4, 2)), dma((4, 2)), dma((32, 2)),
        ],
        compiler_params=pltpu.CompilerParams(
            collective_id=0, has_side_effects=True, vmem_limit_bytes=56 << 20
        ),
        name="gather_project",
    )(feat, wq, wk, wv, ints)


def attention_kernel(
    lists, where_ref, qt, bits, self_score, self_value, kb, vt,
    acc_out, stat_out,
    et, rhs, acc, m, l, kbuf, vbuf, sem, sched, sx, sy,
):
    z = where_ref[0]
    base = where_ref[1]
    lane = lax.broadcasted_iota(I32, (BLK, BLK), 1)
    row = lax.broadcasted_iota(I32, (BLK, BLK), 0)
    for ph in range(15):
        et[ph] = jnp.where((row + 2 * ph) % 30 == lane, 1.0, 0.0).astype(BF)
    et[15] = jnp.where(lane == 31, 1.0, 0.0).astype(BF)

    def phase(g):
        return (4 * ((g // 2) * 8 + 2 * z + g % 2)) % 15

    def build(b, n):
        count = lists[b, 1, SLOTS]

        def inner(t, n):
            first = lists[b, 1, 2 * t]
            live = 2 * t + 1 < count
            second = jnp.where(live, lists[b, 1, jnp.minimum(2 * t + 1, SLOTS - 1)], first)
            sched[0, n] = b
            sched[1, n] = first
            sched[2, n] = second
            sched[3, n] = phase(first)
            sched[4, n] = jnp.where(live, phase(second), 15)
            return n + 1

        return lax.fori_loop(0, (count + 1) // 2, inner, n)

    steps = lax.fori_loop(0, 8, build, 0)
    for extra in range(2):
        for f in range(5):
            sched[f, steps + extra] = 15 if f >= 3 else 0
    even = 2 * ((steps + 1) // 2)

    def copies(i):
        slot = lax.rem(i, NBUF)
        a, b = sched[1, i], sched[2, i]
        return [
            pltpu.make_async_copy(kb.at[a], kbuf.at[slot, 0], sem.at[slot, 0]),
            pltpu.make_async_copy(kb.at[b], kbuf.at[slot, 1], sem.at[slot, 1]),
            pltpu.make_async_copy(vt.at[a], vbuf.at[slot, 0], sem.at[slot, 2]),
            pltpu.make_async_copy(vt.at[b], vbuf.at[slot, 1], sem.at[slot, 3]),
        ]

    for i in range(NBUF - 1):

        @pl.when(i <= even)
        def _():
            for copy in copies(i):
                copy.start()

    def prepare(b, carry):
        brow = bits[b, 0:1, :]
        rr = lax.broadcasted_iota(I32, (32, BLK), 0)
        on = (jnp.broadcast_to(brow, (32, BLK)) >> rr) & 1
        g = jnp.where(on == 1, 0.0, OUT_MASK)
        g = jnp.where(rr < 30, g, jnp.where(rr == 31, OUT_MASK, 0.0)).astype(BF)
        gg = jnp.concatenate([g, g], 1)
        z64 = jnp.zeros((HD, BLK), BF)
        for p in range(4):
            rhs[b, p, 0:64, 0:128] = qt[b, 128 * p : 128 * p + 64, :]
            rhs[b, p, 0:64, 128:256] = z64
            rhs[b, p, 64:128, 0:128] = z64
            rhs[b, p, 64:128, 128:256] = qt[b, 128 * p + 64 : 128 * p + 128, :]
            rhs[b, p, 128:160, :] = gg
            rhs[b, p, 160:256, :] = jnp.zeros((96, 256), BF)
        m[b] = jnp.full((HEADS, BLK), FLOOR, F32)
        l[b] = jnp.zeros((HEADS, BLK), F32)
        acc[b] = jnp.zeros((WIDTH, BLK), F32)
        return carry

    lax.fori_loop(0, 8, prepare, 0)
    for cc in range(2):
        b = 2 * z + cc
        start = where_ref[2 + cc] * BLK
        lanes = lax.broadcasted_iota(I32, (1, BLK), 1)
        on = (bits[b, 0:1, :] >> ((start + lanes) % 30)) & 1
        extra = jnp.broadcast_to(on, (HEADS, BLK)) == 0
        m[b] = jnp.where(extra, self_score[cc], FLOOR)
        l[b] = jnp.where(extra, 1.0, 0.0)
        acc[b] = jnp.where(
            jnp.broadcast_to(on, (WIDTH, BLK)) == 0, self_value[cc].astype(F32), 0.0
        )

    def scores(i, out, p):
        slot = lax.rem(i, NBUF)
        e0, e1, b = et[sched[3, i]], et[sched[4, i]], sched[0, i]
        k0 = kbuf[slot, 0, :, 128 * p : 128 * p + 128]
        k1 = kbuf[slot, 1, :, 128 * p : 128 * p + 128]
        lhs = jnp.concatenate([jnp.concatenate([k0, e0], 1), jnp.concatenate([k1, e1], 1)], 0)
        out[p] = jnp.dot(lhs, rhs[b, p], preferred_element_type=F32)

    def head(i, cur, h):
        slot, b = lax.rem(i, NBUF), sched[0, i]
        p, side = h // 2, h % 2
        old = m[b, h : h + 1, :]
        s = cur[p, :, 128 * side : 128 * side + 128]
        top = jnp.maximum(old, jnp.max(s, axis=0, keepdims=True))
        factor = jnp.exp(old - top)
        w = jnp.exp(cur[p, :, 128 * side : 128 * side + 128] - top)
        m[b, h : h + 1, :] = top
        l[b, h : h + 1, :] = l[b, h : h + 1, :] * factor + jnp.sum(w, axis=0, keepdims=True)
        rows = slice(64 * h, 64 * h + 64)
        v = jnp.concatenate([vbuf[slot, 0, rows, :], vbuf[slot, 1, rows, :]], 1)
        o = jnp.dot(v, w.astype(BF), preferred_element_type=F32)
        acc[b, rows, :] = acc[b, rows, :] * factor + o

    def wait(i):
        for copy in copies(i):
            copy.wait()

    def step(i, cur, nxt):
        @pl.when(i + NBUF - 1 <= even)
        def _():
            for copy in copies(i + NBUF - 1):
                copy.start()

        wait(i + 1)
        for p in range(4):
            scores(i + 1, nxt, p)
            head(i, cur, 2 * p)
            head(i, cur, 2 * p + 1)

    wait(0)
    for p in range(4):
        scores(0, sx, p)

    def body(j, carry):
        step(2 * j, sx, sy)
        step(2 * j + 1, sy, sx)
        return carry

    lax.fori_loop(0, even // 2, body, 0)
    acc_out[...] = acc[...].astype(BF)
    stat_out[:, 0:8, :] = m[...]
    stat_out[:, 8:16, :] = l[...]


def attention_call(ints, where, qt, self_score, self_value, kb, vt):
    vm = pl.BlockSpec(memory_space=pltpu.VMEM)
    sm = pl.BlockSpec(memory_space=pltpu.SMEM)
    anyw = pl.BlockSpec(memory_space=pl.ANY)
    return pl.pallas_call(
        attention_kernel,
        out_shape=(
            jax.ShapeDtypeStruct((8, WIDTH, BLK), BF),
            jax.ShapeDtypeStruct((8, 16, BLK), F32),
        ),
        in_specs=[sm, sm, vm, vm, vm, vm, anyw, anyw],
        out_specs=(vm, vm),
        scratch_shapes=[
            pltpu.VMEM((16, BLK, BLK), BF),
            pltpu.VMEM((8, 4, 256, 256), BF),
            pltpu.VMEM((8, WIDTH, BLK), F32),
            pltpu.VMEM((8, HEADS, BLK), F32),
            pltpu.VMEM((8, HEADS, BLK), F32),
            pltpu.VMEM((NBUF, 2, BLK, WIDTH), BF),
            pltpu.VMEM((NBUF, 2, WIDTH, BLK), BF),
            pltpu.SemaphoreType.DMA((NBUF, 4)),
            pltpu.SMEM((5, 136), I32),
            pltpu.VMEM((4, 256, 256), F32),
            pltpu.VMEM((4, 256, 256), F32),
        ],
        compiler_params=pltpu.CompilerParams(vmem_limit_bytes=56 << 20),
        name="block_attention",
    )(ints, where, qt, ints, self_score, self_value, kb, vt)


def merge_kernel(
    acc, stat, dq, ids, w_out,
    updated_out, pooled_out,
    acc_got, stat_got, made, mine, part, ring_part, total, all_part,
    a_send, a_recv, s_send, s_recv, u_send, u_recv, r_send, r_recv, g_send, g_recv,
):
    x, y, c, z = place()
    me = dst_index(x, y, c)
    ring = []
    for dy in range(4):
        for dc in range(2):
            if dy or dc:
                ring.append((dy, dc, (dst_index(x, y + dy, flip(c, dc)), z)))
    far = []
    for dx in range(4):
        for dz in range(4):
            if dx or dz:
                far.append((dx, dz, (dst_index(x + dx, y, c), (z + dz) % 4)))
    barrier = pltpu.get_barrier_semaphore()
    for _, _, peer in ring + far:
        pl.semaphore_signal(barrier, inc=1, device_id=peer, device_id_type=MESH)
    pl.semaphore_wait(barrier, len(ring) + len(far))

    def remote(src, dst, send, recv, to):
        return pltpu.make_async_remote_copy(
            src_ref=src, dst_ref=dst, send_sem=send, recv_sem=recv, device_id=to, device_id_type=MESH
        )

    sent = []

    def go(copy):
        copy.start()
        sent.append(copy)

    for dz in (2, 1, 3):
        to = (z + dz) % 4
        rows = pl.ds(2 * to, 2)
        go(remote(acc.at[rows], acc_got.at[dz - 1], a_send.at[dz - 1], a_recv.at[dz - 1], (me, to)))
        go(remote(stat.at[rows], stat_got.at[dz - 1], s_send.at[dz - 1], s_recv.at[dz - 1], (me, to)))
    for dz in (1, 3, 2):
        rows = pl.ds(2 * z, 2)
        remote(acc.at[rows], acc_got.at[dz - 1], a_send.at[dz - 1], a_recv.at[dz - 1], (me, z)).wait_recv()
        remote(stat.at[rows], stat_got.at[dz - 1], s_send.at[dz - 1], s_recv.at[dz - 1], (me, z)).wait_recv()
    yy = (z - y + 4) % 4
    for cc in range(2):
        b = 2 * z + cc
        stats = [stat[b]] + [stat_got[k, cc] for k in range(3)]
        top = stats[0][0:8]
        for s in stats[1:]:
            top = jnp.maximum(top, s[0:8])
        factors = [jnp.exp(s[0:8] - top) for s in stats]
        whole = sum(f * s[8:16] for f, s in zip(factors, stats))
        inv = 1.0 / whole
        factors = [f * inv for f in factors]
        pieces = []
        for h in range(HEADS):
            rows = slice(64 * h, 64 * h + 64)
            o = acc[b, rows, :].astype(F32) * factors[0][h : h + 1, :]
            for k in range(3):
                o = o + acc_got[k, cc, rows, :].astype(F32) * factors[k + 1][h : h + 1, :]
            pieces.append(o)
        att = jnp.concatenate(pieces, 0).T.astype(BF)
        mixed = jnp.dot(att, w_out[...], preferred_element_type=F32)
        new = (dq[cc].astype(F32) + mixed).astype(BF)
        made[cc] = new
        gid = ids[b, 2:3, :]
        member = jnp.where(
            jnp.broadcast_to(gid, (8, BLK)) == lax.broadcasted_iota(I32, (8, BLK), 0), 1.0, 0.0
        )
        sums = jnp.dot(member.astype(BF), new, preferred_element_type=F32)
        counts = jnp.broadcast_to(jnp.sum(member, axis=1, keepdims=True), (8, BLK))
        both = jnp.concatenate([sums, counts], 1)
        part[...] = both if cc == 0 else part[...] + both
    for cc in range(2):
        own = jnp.logical_and(yy == y, c == cc)
        half = flip(c, cc)
        copy = remote(made.at[cc], mine.at[half], u_send.at[cc], u_recv.at[half], (dst_index(x, yy, cc), z))
        local = pltpu.make_async_copy(made.at[cc], mine.at[half], u_recv.at[half])
        pl.when(jnp.logical_not(own))(copy.start)
        pl.when(own)(local.start)
    for dy, dc, to in ring:
        k = 2 * dy + dc
        go(remote(part, ring_part.at[k], r_send.at[k], r_recv.at[k], to))
    whole = part[...]
    for dy, dc, to in ring:
        k = 2 * dy + dc
        remote(part, ring_part.at[k], r_send.at[k], r_recv.at[k], to).wait_recv()
        whole = whole + ring_part[k]
    total[...] = whole
    for dx, dz, to in far:
        k = 4 * dx + dz
        go(remote(total, all_part.at[k], g_send.at[k], g_recv.at[k], to))
    for half in range(2):
        pltpu.make_async_copy(made.at[half], mine.at[half], u_recv.at[half]).wait()
    updated_out[0:BLK, :] = mine[0]
    updated_out[BLK:ROWS, :] = mine[1]
    for dx, dz, to in far:
        k = 4 * dx + dz
        remote(total, all_part.at[k], g_send.at[k], g_recv.at[k], to).wait_recv()
        whole = whole + all_part[k]
    scale = 1.0 / jnp.sqrt(jnp.concatenate([whole[0:4, WIDTH:]] * 4, 1))
    pooled_out[...] = whole[0:4, :WIDTH] * scale
    for cc in range(2):
        own = jnp.logical_and(yy == y, c == cc)
        copy = remote(
            made.at[cc], mine.at[flip(c, cc)], u_send.at[cc], u_recv.at[flip(c, cc)],
            (dst_index(x, yy, cc), z),
        )
        pl.when(jnp.logical_not(own))(copy.wait_send)
    for copy in sent:
        copy.wait_send()


def merge_call(acc, stat, dq, ids, w_out):
    vm = pl.BlockSpec(memory_space=pltpu.VMEM)
    dma = pltpu.SemaphoreType.DMA
    return pl.pallas_call(
        merge_kernel,
        out_shape=(
            jax.ShapeDtypeStruct((ROWS, WIDTH), BF),
            jax.ShapeDtypeStruct((4, WIDTH), F32),
        ),
        in_specs=[vm] * 5,
        out_specs=(vm, vm),
        scratch_shapes=[
            pltpu.VMEM((3, 2, WIDTH, BLK), BF),
            pltpu.VMEM((3, 2, 16, BLK), F32),
            pltpu.VMEM((2, BLK, WIDTH), BF),
            pltpu.VMEM((2, BLK, WIDTH), BF),
            pltpu.VMEM((8, WIDTH + BLK), F32),
            pltpu.VMEM((8, 8, WIDTH + BLK), F32),
            pltpu.VMEM((8, WIDTH + BLK), F32),
            pltpu.VMEM((16, 8, WIDTH + BLK), F32),
            dma((3,)), dma((3,)), dma((3,)), dma((3,)), dma((2,)), dma((2,)),
            dma((8,)), dma((8,)), dma((16,)), dma((16,)),
        ],
        compiler_params=pltpu.CompilerParams(
            collective_id=1, has_side_effects=True, vmem_limit_bytes=40 << 20
        ),
        name="merge_project_pool",
    )(acc, stat, dq, ids, w_out)


def shards(features, w_query, w_key, w_value, w_out, node_bits, block_src, block_count, graph_ids):
    x, y, c, z = place()
    bits = node_bits.reshape(8, 1, BLK)
    slots = jnp.concatenate(
        [block_src, jnp.broadcast_to(block_count[:, :, None], (8, 1, BLK - SLOTS))], axis=2
    )
    ids = jnp.tile(graph_ids.reshape(2, 1, BLK), (4, 1, 1))
    ints = jnp.concatenate([bits, slots, ids, jnp.zeros((8, 5, BLK), I32)], axis=1)
    kb, vt, qt, got, dq, self_score, self_value = gather_call(features, w_query, w_key, w_value, ints)
    yy = (z - y + 4) % 4
    own = [dst_index(x, yy, cc) * 8 + 2 * z + flip(c, cc) for cc in range(2)]
    where = jnp.stack([z, z, own[0], own[1]]).astype(I32)
    acc, stat = attention_call(
        got, where, qt, self_score, self_value, kb.reshape(64, BLK, WIDTH), vt.reshape(64, WIDTH, BLK)
    )
    return merge_call(acc, stat, dq, got, w_out)


def solution(mesh):
    placed = (
        P(("dst", "src"), None),
        P(),
        P(),
        P(),
        P(),
        P("dst"),
        P("dst", "src", None),
        P("dst", "src"),
        P(("dst", "src")),
    )
    return jax.shard_map(
        shards,
        mesh=mesh,
        in_specs=placed,
        out_specs=(P(("dst", "src"), None), P()),
        check_vma=False,
    )
```

```python
import functools

import jax
import jax.numpy as jnp
from jax import lax
from jax.experimental import pallas as pl
from jax.experimental.pallas import tpu as pltpu
from jax.sharding import PartitionSpec as P

MESH = pl.DeviceIdType.MESH
BF, F32, I32 = jnp.bfloat16, jnp.float32, jnp.int32
WIDTH, HEADS, HD, BLK, ROWS = 512, 8, 64, 128, 256
SLOTS = 32
OUT_MASK = -3e38
FLOOR = -1e30
RING = 4


def place():
    d = lax.axis_index("dst")
    return d // 8, (d // 2) % 4, d % 2, lax.axis_index("src")


def dst_index(x, y, core):
    return (x % 4) * 8 + (y % 4) * 2 + core


def flip(a, b):
    return a + b - 2 * a * b


def nt(a, b):
    return lax.dot_general(a, b, (((1,), (1,)), ((), ())), preferred_element_type=F32)


def gather_kernel(
    feat, wq_hbm, wk_hbm, wv_hbm, bits, slots, counts, ids,
    kb, vt, q_out, ints_out, dq_out, self_score, self_value,
    fbuf, wq, wk, wv, wqt, wkt, wvt, dq, ints, got,
    ring_send, ring_recv, sib_send, sib_recv, z_send, z_recv, i_send, i_recv, in_sem,
):
    x, y, c, z = place()
    me = dst_index(x, y, c)
    sibling = dst_index(x, y, 1 - c)

    def blk(core, i, j):
        return dst_index(x + (1 - core) * i + core * j, y + core * i + (1 - core) * j, core)

    zup, zdown = (z + 1) % 4, (z + 3) % 4
    peers = [(dst_index(x + 1, y, c), z), (dst_index(x + 3, y, c), z), (me, zup), (me, zdown)]
    for dy in range(4):
        for dc in range(2):
            if dy or dc:
                peers.append((dst_index(x, y + dy, flip(c, dc)), z))
    barrier = pltpu.get_barrier_semaphore()
    for peer in peers:
        pl.semaphore_signal(barrier, inc=1, device_id=peer, device_id_type=MESH)
    loads = [
        pltpu.make_async_copy(src, dst, in_sem.at[n])
        for n, (src, dst) in enumerate(((feat, fbuf.at[me]), (wv_hbm, wv), (wk_hbm, wk), (wq_hbm, wq)))
    ]
    for copy in loads:
        copy.start()
    for b in range(8):
        ints[b] = jnp.zeros((8, BLK), I32)
        ints[b, 0:1, :] = bits[b : b + 1, :]
        ints[b, 1:2, 0:SLOTS] = slots[b]
        ints[b, 2:3, :] = ids[b % 2 : b % 2 + 1, :]
        ints[b, 3:4, :] = jnp.broadcast_to(counts[b : b + 1, :], (1, BLK))
    loads[0].wait()
    pl.semaphore_wait(barrier, len(peers))

    def remote(src, dst, send, recv, to):
        return pltpu.make_async_remote_copy(
            src_ref=src, dst_ref=dst, send_sem=send, recv_sem=recv, device_id=to, device_id_type=MESH
        )

    sent = []

    def go(copy):
        copy.start()
        sent.append(copy)

    legs = ((3, 0, 1), (3, 1, 1), (1, 1, 3), (1, 0, 3), (2, 0, 1), (2, 1, 3))

    def half_ref(row, at, part):
        b = blk(c, at, 0) if row == 0 else blk(c, row - 1, at)
        return fbuf.at[b, pl.ds(part * BLK, BLK)]

    def leg(row, n, at):
        _, part, step = legs[n]
        to = blk(c, step, 0) if row == 0 else blk(c, 0, step)
        r = half_ref(row, at, part)
        return remote(r, r, ring_send.at[row, n], ring_recv.at[row, n], (to, z))

    def spread(row):
        for n in (0, 2, 1, 3):
            go(leg(row, n, 0))

    def arrive(row, *ns):
        for n in ns:
            leg(row, n, legs[n][0]).wait_recv()

    def forward(row):
        arrive(row, 0)
        go(leg(row, 4, 3))
        arrive(row, 2)
        go(leg(row, 5, 1))

    def share(*places):
        for i, j in places:
            b = blk(c, i, j)
            go(remote(fbuf.at[b], fbuf.at[b], sib_send.at[i, j], sib_recv.at[i, j], (sibling, z)))

    def shared(*places):
        for i, j in places:
            b = blk(1 - c, i, j)
            remote(fbuf.at[b], fbuf.at[b], sib_send.at[i, j], sib_recv.at[i, j], (sibling, z)).wait_recv()

    def project(b):
        f = fbuf[b]
        kb[b] = jnp.dot(f, wk[...], preferred_element_type=F32).astype(BF)
        v = nt(wvt[...], f).astype(BF)
        vt[b, 0] = v[:, :BLK]
        vt[b, 1] = v[:, BLK:]

    def project_many(core, *places):
        code = 0
        for i, j in reversed(places):
            code = code * 16 + 4 * i + j

        def body(e, code):
            project(blk(core, code % 16 // 4, code % 4))
            return code // 16

        lax.fori_loop(0, len(places), body, jnp.int32(code))

    spread(0)
    spread(1)
    share((0, 0))
    for dy in range(4):
        for dc in range(2):
            s = (2 * y + dy) % 4
            src = ints.at[2 * s + dc]
            slot = 2 * s + c
            if dy == 0 and dc == 0:
                local_ints = pltpu.make_async_copy(src, got.at[slot], i_recv.at[dy, dc])
                local_ints.start()
            else:
                go(
                    remote(
                        src, got.at[slot], i_send.at[dy, dc], i_recv.at[dy, dc],
                        (dst_index(x, y + dy, flip(c, dc)), z),
                    )
                )
    for copy in loads[1:]:
        copy.wait()
    wvt[...] = wv[...].T
    wqt[...] = wq[...].T
    wkt[...] = wk[...].T

    forward(0)
    forward(1)
    project(me)
    arrive(0, 1, 3)
    spread(4)
    spread(2)
    share((3, 0), (1, 0))
    arrive(1, 1, 3)
    share((0, 3), (0, 1))
    shared((0, 0))
    project(sibling)
    arrive(0, 4, 5)
    spread(3)
    share((2, 0))
    arrive(1, 4, 5)
    share((0, 2))
    project_many(c, (1, 0), (3, 0), (0, 1))
    shared((1, 0), (3, 0), (0, 1), (0, 3), (2, 0), (0, 2))

    yy = (z - y + 4) % 4

    def plane_rows(cc):
        return fbuf.at[dst_index(x, yy, cc), pl.ds(pl.multiple_of(flip(c, cc) * BLK, BLK), BLK)]

    for first in range(2):
        for up, to in ((0, zup), (1, zdown)):
            cc = flip(first, up)
            go(remote(plane_rows(cc), dq.at[z, cc], z_send.at[up, cc], z_recv.at[up, cc], (me, to)))
    own_copies = [pltpu.make_async_copy(plane_rows(cc), dq.at[z, cc], z_recv.at[3, cc]) for cc in range(2)]
    for copy in own_copies:
        copy.start()

    forward(4)
    forward(2)
    project_many(c, (0, 3), (2, 0), (0, 2))
    arrive(4, 1, 3)
    share((3, 3), (3, 1))
    arrive(2, 1, 3)
    share((1, 3), (1, 1))
    project_many(1 - c, (1, 0), (3, 0))
    forward(3)

    def z_leg(up, cc, frm):
        return remote(dq.at[frm, cc], dq.at[frm, cc], z_send.at[up, cc], z_recv.at[up, cc], (me, zup))

    z_leg(0, 0, zdown).wait_recv()
    go(remote(dq.at[zdown, 0], dq.at[zdown, 0], z_send.at[2, 0], z_recv.at[2, 0], (me, zup)))
    z_leg(1, 1, zup).wait_recv()
    go(remote(dq.at[zup, 1], dq.at[zup, 1], z_send.at[2, 1], z_recv.at[2, 1], (me, zdown)))
    project_many(1 - c, (0, 1), (0, 3), (2, 0), (0, 2))
    project_many(c, (1, 1), (1, 3), (3, 1), (3, 3))
    for copy in own_copies:
        copy.wait()

    def query(s, cc):
        q = nt(wqt[...], dq[s, cc]).astype(BF)
        q_out[2 * s + cc] = q * 0.125

    def queries(e, carry):
        query((z + 3 + e // 2) % 4, e % 2)
        return carry

    z_leg(0, 1, zdown).wait_recv()
    z_leg(1, 0, zup).wait_recv()
    arrive(4, 4, 5)
    share((3, 2))
    arrive(2, 4, 5)
    share((1, 2))
    shared((1, 1), (1, 3), (3, 1), (3, 3))
    project_many(1 - c, (1, 1), (1, 3), (3, 1), (3, 3))
    lax.fori_loop(0, 6, queries, 0)
    for cc in range(2):
        f = dq[z, cc]
        dq_out[cc] = f
        k = nt(wkt[...], f).astype(BF).astype(F32)
        q = q_out[2 * z + cc].astype(F32)
        prod = k * q
        self_score[cc] = jnp.concatenate(
            [jnp.sum(prod[h * HD : (h + 1) * HD], axis=0, keepdims=True) for h in range(HEADS)], axis=0
        )
        self_value[cc] = nt(wvt[...], f).astype(BF)
    local_ints.wait()
    for dy in range(4):
        for dc in range(2):
            if dy or dc:
                slot = 2 * ((2 * y + 4 - dy) % 4) + flip(c, dc)
                remote(
                    got.at[slot], got.at[slot], i_send.at[dy, dc], i_recv.at[dy, dc], (sibling, z)
                ).wait_recv()
    ints_out[...] = got[...]
    project_many(c, (1, 2), (3, 2))
    arrive(3, 1, 3)
    share((2, 3), (2, 1))
    far = (z + 2) % 4
    for cc in range(2):
        z_leg(2, cc, far).wait_recv()
    for cc in range(2):
        query(far, cc)
    shared((1, 2), (3, 2))
    project_many(1 - c, (1, 2), (3, 2))
    project_many(c, (2, 1), (2, 3))
    arrive(3, 4, 5)
    share((2, 2))
    project_many(c, (2, 2))
    shared((2, 1), (2, 3), (2, 2))
    project_many(1 - c, (2, 1), (2, 3), (2, 2))
    for copy in sent:
        copy.wait_send()


def gather_call(*args):
    hbm = pl.BlockSpec(memory_space=pltpu.HBM)
    vm = pl.BlockSpec(memory_space=pltpu.VMEM)
    dma = pltpu.SemaphoreType.DMA
    return pl.pallas_call(
        gather_kernel,
        out_shape=(
            pltpu.VMEM((32, ROWS, WIDTH), BF),
            pltpu.VMEM((32, 2, WIDTH, BLK), BF),
            pltpu.VMEM((8, WIDTH, BLK), BF),
            jax.ShapeDtypeStruct((8, 8, BLK), I32),
            pltpu.VMEM((2, BLK, WIDTH), BF),
            pltpu.VMEM((2, HEADS, BLK), F32),
            pltpu.VMEM((2, WIDTH, BLK), BF),
        ),
        in_specs=[hbm] * 4 + [vm] * 4,
        out_specs=(vm,) * 7,
        scratch_shapes=[
            pltpu.VMEM((32, ROWS, WIDTH), BF),
            *[pltpu.VMEM((WIDTH, WIDTH), BF)] * 6,
            pltpu.VMEM((4, 2, BLK, WIDTH), BF),
            pltpu.VMEM((8, 8, BLK), I32),
            pltpu.VMEM((8, 8, BLK), I32),
            dma((5, 6)), dma((5, 6)), dma((4, 4)), dma((4, 4)),
            dma((3, 2)), dma((4, 2)), dma((4, 2)), dma((4, 2)), dma((4,)),
        ],
        compiler_params=pltpu.CompilerParams(
            collective_id=0, has_side_effects=True, vmem_limit_bytes=44 << 20
        ),
        name="gather_project",
    )(*args)


def attention_kernel(
    lists, qt, bits, self_score, self_value, kb, vt,
    acc_out, stat_out,
    et, rhs, acc, m, l, sched, sx, sy, mx, my,
):
    x, y, c, z = place()
    lane = lax.broadcasted_iota(I32, (BLK, BLK), 1)
    row = lax.broadcasted_iota(I32, (BLK, BLK), 0)
    for ph in range(15):
        et[ph] = jnp.where((row + 2 * ph) % 30 == lane, 1.0, 0.0).astype(BF)
    et[15] = jnp.where(lane == 31, 1.0, 0.0).astype(BF)

    def phase(g):
        return (4 * ((g // 2) * 8 + 2 * z + g % 2)) % 15

    def build(b, n):
        count = lists[b, 3, 0]

        def inner(t, n):
            first = lists[b, 1, 2 * t]
            live = 2 * t + 1 < count
            second = jnp.where(live, lists[b, 1, jnp.minimum(2 * t + 1, SLOTS - 1)], first)
            sched[0, n] = b
            sched[1, n] = first
            sched[2, n] = second
            sched[3, n] = phase(first)
            sched[4, n] = jnp.where(live, phase(second), 15)
            return n + 1

        return lax.fori_loop(0, (count + 1) // 2, inner, n)

    steps = lax.fori_loop(0, 8, build, 0)
    for extra in range(2):
        for f in range(5):
            sched[f, steps + extra] = 15 if f >= 3 else 0
    even = 2 * ((steps + 1) // 2)

    def prepare(b, carry):
        brow = bits[b, 0:1, :]
        rr = lax.broadcasted_iota(I32, (32, BLK), 0)
        on = (jnp.broadcast_to(brow, (32, BLK)) >> rr) & 1
        g = jnp.where(on == 1, 0.0, OUT_MASK)
        g = jnp.where(rr < 30, g, jnp.where(rr == 31, OUT_MASK, 0.0)).astype(BF)
        gg = jnp.concatenate([g, g], 1)
        z64 = jnp.zeros((HD, BLK), BF)
        for p in range(4):
            rhs[b, p, 0:64, 0:128] = qt[b, 128 * p : 128 * p + 64, :]
            rhs[b, p, 0:64, 128:256] = z64
            rhs[b, p, 64:128, 0:128] = z64
            rhs[b, p, 64:128, 128:256] = qt[b, 128 * p + 64 : 128 * p + 128, :]
            rhs[b, p, 128:160, :] = gg
            rhs[b, p, 160:256, :] = jnp.zeros((96, 256), BF)
        m[b] = jnp.full((HEADS, BLK), FLOOR, F32)
        l[b] = jnp.zeros((HEADS, BLK), F32)
        acc[b] = jnp.zeros((WIDTH, BLK), F32)
        return carry

    lax.fori_loop(0, 8, prepare, 0)
    for cc in range(2):
        b = 2 * z + cc
        start = (dst_index(x, z - y + 4, cc) * 8 + 2 * z + flip(c, cc)) * BLK
        lanes = lax.broadcasted_iota(I32, (1, BLK), 1)
        on = (bits[b, 0:1, :] >> ((start + lanes) % 30)) & 1
        extra = jnp.broadcast_to(on, (HEADS, BLK)) == 0
        m[b] = jnp.where(extra, self_score[cc], FLOOR)
        l[b] = jnp.where(extra, 1.0, 0.0)
        acc[b] = jnp.where(
            jnp.broadcast_to(on, (WIDTH, BLK)) == 0, self_value[cc].astype(F32), 0.0
        )

    def scores(i, out, tops, p):
        e0, e1, b = et[sched[3, i]], et[sched[4, i]], sched[0, i]
        cols = slice(128 * p, 128 * p + 128)
        k0, k1 = kb[sched[1, i], :, cols], kb[sched[2, i], :, cols]
        lhs = jnp.concatenate([jnp.concatenate([k0, e0], 1), jnp.concatenate([k1, e1], 1)], 0)
        s = jnp.dot(lhs, rhs[b, p], preferred_element_type=F32)
        out[p] = s
        top = jnp.max(s.reshape(32, 8, 256), axis=0)
        tops[2 * p] = top[:, :128]
        tops[2 * p + 1] = top[:, 128:]

    def head(i, cur, tops, h):
        b = sched[0, i]
        p, side = h // 2, h % 2
        old = m[b, h : h + 1, :]
        top = jnp.maximum(old, jnp.max(tops[h], axis=0, keepdims=True))
        factor = jnp.exp(old - top)
        w = jnp.exp(cur[p, :, 128 * side : 128 * side + 128] - top)
        m[b, h : h + 1, :] = top
        l[b, h : h + 1, :] = l[b, h : h + 1, :] * factor + jnp.sum(w, axis=0, keepdims=True)
        rows = slice(64 * h, 64 * h + 64)
        v = jnp.concatenate([vt[sched[1, i], rows, :], vt[sched[2, i], rows, :]], 1)
        o = jnp.dot(v, w.astype(BF), preferred_element_type=F32)
        acc[b, rows, :] = acc[b, rows, :] * factor + o

    def step(i, cur, tops, nxt, next_tops):
        for p in range(4):
            scores(i + 1, nxt, next_tops, p)
            head(i, cur, tops, 2 * p)
            head(i, cur, tops, 2 * p + 1)

    for p in range(4):
        scores(0, sx, mx, p)

    def body(j, carry):
        step(2 * j, sx, mx, sy, my)
        step(2 * j + 1, sy, my, sx, mx)
        return carry

    lax.fori_loop(0, even // 2, body, 0)
    acc_out[...] = acc[...].astype(BF)
    stat_out[:, 0:8, :] = m[...]
    stat_out[:, 8:16, :] = l[...]


def attention_call(ints, qt, self_score, self_value, kb, vt):
    vm = pl.BlockSpec(memory_space=pltpu.VMEM)
    sm = pl.BlockSpec(memory_space=pltpu.SMEM)
    return pl.pallas_call(
        attention_kernel,
        out_shape=(
            pltpu.VMEM((8, WIDTH, BLK), BF),
            pltpu.VMEM((8, 16, BLK), F32),
        ),
        in_specs=[sm, vm, vm, vm, vm, vm, vm],
        out_specs=(vm, vm),
        scratch_shapes=[
            pltpu.VMEM((16, BLK, BLK), BF),
            pltpu.VMEM((8, 4, 256, 256), BF),
            pltpu.VMEM((8, WIDTH, BLK), F32),
            pltpu.VMEM((8, HEADS, BLK), F32),
            pltpu.VMEM((8, HEADS, BLK), F32),
            pltpu.SMEM((5, 136), I32),
            pltpu.VMEM((4, 256, 256), F32),
            pltpu.VMEM((4, 256, 256), F32),
            pltpu.VMEM((8, 8, BLK), F32),
            pltpu.VMEM((8, 8, BLK), F32),
        ],
        compiler_params=pltpu.CompilerParams(vmem_limit_bytes=24 << 20),
        name="block_attention",
    )(ints, qt, ints, self_score, self_value, kb, vt)


def merge_kernel(
    acc, stat, dq, ids, w_out,
    updated_out, pooled_out,
    acc_got, stat_got, made, mine, part, ring_part, total, all_part,
    a_send, a_recv, s_send, s_recv, u_send, u_recv, r_send, r_recv, g_send, g_recv,
):
    x, y, c, z = place()
    me = dst_index(x, y, c)
    ring = []
    for dy in range(4):
        for dc in range(2):
            if dy or dc:
                ring.append((dy, dc, (dst_index(x, y + dy, flip(c, dc)), z)))
    far = []
    for dx in range(4):
        for dz in range(4):
            if dx or dz:
                far.append((dx, dz, (dst_index(x + dx, y, c), (z + dz) % 4)))
    barrier = pltpu.get_barrier_semaphore()
    for _, _, peer in ring + far:
        pl.semaphore_signal(barrier, inc=1, device_id=peer, device_id_type=MESH)
    pl.semaphore_wait(barrier, len(ring) + len(far))

    def remote(src, dst, send, recv, to):
        return pltpu.make_async_remote_copy(
            src_ref=src, dst_ref=dst, send_sem=send, recv_sem=recv, device_id=to, device_id_type=MESH
        )

    sent = []

    def go(copy):
        copy.start()
        sent.append(copy)

    for dz in (2, 1, 3):
        to = (z + dz) % 4
        rows = pl.ds(2 * to, 2)
        go(remote(acc.at[rows], acc_got.at[dz - 1], a_send.at[dz - 1], a_recv.at[dz - 1], (me, to)))
        go(remote(stat.at[rows], stat_got.at[dz - 1], s_send.at[dz - 1], s_recv.at[dz - 1], (me, to)))
    for dz in (1, 3, 2):
        rows = pl.ds(2 * z, 2)
        remote(acc.at[rows], acc_got.at[dz - 1], a_send.at[dz - 1], a_recv.at[dz - 1], (me, z)).wait_recv()
        remote(stat.at[rows], stat_got.at[dz - 1], s_send.at[dz - 1], s_recv.at[dz - 1], (me, z)).wait_recv()
    yy = (z - y + 4) % 4
    for cc in range(2):
        b = 2 * z + cc
        stats = [stat[b]] + [stat_got[k, cc] for k in range(3)]
        top = stats[0][0:8]
        for s in stats[1:]:
            top = jnp.maximum(top, s[0:8])
        factors = [jnp.exp(s[0:8] - top) for s in stats]
        whole = sum(f * s[8:16] for f, s in zip(factors, stats))
        inv = 1.0 / whole
        factors = [f * inv for f in factors]
        pieces = []
        for h in range(HEADS):
            rows = slice(64 * h, 64 * h + 64)
            o = acc[b, rows, :].astype(F32) * factors[0][h : h + 1, :]
            for k in range(3):
                o = o + acc_got[k, cc, rows, :].astype(F32) * factors[k + 1][h : h + 1, :]
            pieces.append(o)
        att = jnp.concatenate(pieces, 0).T.astype(BF)
        mixed = jnp.dot(att, w_out[...], preferred_element_type=F32)
        new = (dq[cc].astype(F32) + mixed).astype(BF)
        made[cc] = new
        gid = ids[b, 2:3, :]
        member = jnp.where(
            jnp.broadcast_to(gid, (8, BLK)) == lax.broadcasted_iota(I32, (8, BLK), 0), 1.0, 0.0
        )
        sums = jnp.dot(member.astype(BF), new, preferred_element_type=F32)
        counts = jnp.broadcast_to(jnp.sum(member, axis=1, keepdims=True), (8, BLK))
        both = jnp.concatenate([sums, counts], 1)
        part[...] = both if cc == 0 else part[...] + both
    for cc in range(2):
        own = jnp.logical_and(yy == y, c == cc)
        half = flip(c, cc)
        copy = remote(made.at[cc], mine.at[half], u_send.at[cc], u_recv.at[half], (dst_index(x, yy, cc), z))
        local = pltpu.make_async_copy(made.at[cc], mine.at[half], u_recv.at[half])
        pl.when(jnp.logical_not(own))(copy.start)
        pl.when(own)(local.start)
    for dy, dc, to in ring:
        k = 2 * dy + dc
        go(remote(part, ring_part.at[k], r_send.at[k], r_recv.at[k], to))
    whole = part[...]
    for dy, dc, to in ring:
        k = 2 * dy + dc
        remote(part, ring_part.at[k], r_send.at[k], r_recv.at[k], to).wait_recv()
        whole = whole + ring_part[k]
    total[...] = whole
    for dx, dz, to in far:
        k = 4 * dx + dz
        go(remote(total, all_part.at[k], g_send.at[k], g_recv.at[k], to))
    for half in range(2):
        pltpu.make_async_copy(made.at[half], mine.at[half], u_recv.at[half]).wait()
    updated_out[0:BLK, :] = mine[0]
    updated_out[BLK:ROWS, :] = mine[1]
    for dx, dz, to in far:
        k = 4 * dx + dz
        remote(total, all_part.at[k], g_send.at[k], g_recv.at[k], to).wait_recv()
        whole = whole + all_part[k]
    scale = 1.0 / jnp.sqrt(jnp.concatenate([whole[0:4, WIDTH:]] * 4, 1))
    pooled_out[...] = whole[0:4, :WIDTH] * scale
    for cc in range(2):
        own = jnp.logical_and(yy == y, c == cc)
        copy = remote(
            made.at[cc], mine.at[flip(c, cc)], u_send.at[cc], u_recv.at[flip(c, cc)],
            (dst_index(x, yy, cc), z),
        )
        pl.when(jnp.logical_not(own))(copy.wait_send)
    for copy in sent:
        copy.wait_send()


def merge_call(acc, stat, dq, ids, w_out):
    vm = pl.BlockSpec(memory_space=pltpu.VMEM)
    dma = pltpu.SemaphoreType.DMA
    return pl.pallas_call(
        merge_kernel,
        out_shape=(
            jax.ShapeDtypeStruct((ROWS, WIDTH), BF),
            jax.ShapeDtypeStruct((4, WIDTH), F32),
        ),
        in_specs=[vm] * 5,
        out_specs=(vm, vm),
        scratch_shapes=[
            pltpu.VMEM((3, 2, WIDTH, BLK), BF),
            pltpu.VMEM((3, 2, 16, BLK), F32),
            pltpu.VMEM((2, BLK, WIDTH), BF),
            pltpu.VMEM((2, BLK, WIDTH), BF),
            pltpu.VMEM((8, WIDTH + BLK), F32),
            pltpu.VMEM((8, 8, WIDTH + BLK), F32),
            pltpu.VMEM((8, WIDTH + BLK), F32),
            pltpu.VMEM((16, 8, WIDTH + BLK), F32),
            dma((3,)), dma((3,)), dma((3,)), dma((3,)), dma((2,)), dma((2,)),
            dma((8,)), dma((8,)), dma((16,)), dma((16,)),
        ],
        compiler_params=pltpu.CompilerParams(
            collective_id=1, has_side_effects=True, vmem_limit_bytes=16 << 20
        ),
        name="merge_project_pool",
    )(acc, stat, dq, ids, w_out)


def shards(features, w_query, w_key, w_value, w_out, node_bits, block_src, block_count, graph_ids):
    kb, vt, qt, got, dq, self_score, self_value = gather_call(
        features, w_query, w_key, w_value,
        node_bits.reshape(8, BLK), block_src, block_count, graph_ids.reshape(2, BLK),
    )
    acc, stat = attention_call(
        got, qt, self_score, self_value, kb.reshape(64, BLK, WIDTH), vt.reshape(64, WIDTH, BLK)
    )
    return merge_call(acc, stat, dq, got, w_out)


def solution(mesh):
    placed = (
        P(("dst", "src"), None),
        P(),
        P(),
        P(),
        P(),
        P("dst"),
        P("dst", "src", None),
        P("dst", "src"),
        P(("dst", "src")),
    )
    return jax.shard_map(
        shards,
        mesh=mesh,
        in_specs=placed,
        out_specs=(P(("dst", "src"), None), P()),
        check_vma=False,
    )
```

```python
import functools

import jax
import jax.numpy as jnp
from jax import lax
from jax.experimental import pallas as pl
from jax.experimental.pallas import tpu as pltpu
from jax.sharding import PartitionSpec as P

MESH = pl.DeviceIdType.MESH
BF, F32, I32 = jnp.bfloat16, jnp.float32, jnp.int32
WIDTH, HEADS, HD, BLK, ROWS = 512, 8, 64, 128, 256
SLOTS = 32
OUT_MASK = -3e38
FLOOR = -1e30
RING = 4


def place():
    d = lax.axis_index("dst")
    return d // 8, (d // 2) % 4, d % 2, lax.axis_index("src")


def dst_index(x, y, core):
    return (x % 4) * 8 + (y % 4) * 2 + core


def flip(a, b):
    return a + b - 2 * a * b


def nt(a, b):
    return lax.dot_general(a, b, (((1,), (1,)), ((), ())), preferred_element_type=F32)


def gather_kernel(
    feat, wq_hbm, wk_hbm, wv_hbm, bits, slots, counts, ids,
    kb, vt, q_out, ints_out, dq_out, self_score, self_value,
    fbuf, wq, wk, wv, wqt, wkt, wvt, dq, ints, got,
    ring_send, ring_recv, sib_send, sib_recv, z_send, z_recv, i_send, i_recv, in_sem,
):
    x, y, c, z = place()
    me = dst_index(x, y, c)
    sibling = dst_index(x, y, 1 - c)

    def blk(core, i, j):
        return dst_index(x + (1 - core) * i + core * j, y + core * i + (1 - core) * j, core)

    zup, zdown = (z + 1) % 4, (z + 3) % 4
    peers = [(dst_index(x + 1, y, c), z), (dst_index(x + 3, y, c), z), (me, zup), (me, zdown)]
    for dy in range(4):
        for dc in range(2):
            if dy or dc:
                peers.append((dst_index(x, y + dy, flip(c, dc)), z))
    barrier = pltpu.get_barrier_semaphore()
    for peer in peers:
        pl.semaphore_signal(barrier, inc=1, device_id=peer, device_id_type=MESH)
    loads = [
        pltpu.make_async_copy(src, dst, in_sem.at[n])
        for n, (src, dst) in enumerate(((feat, fbuf.at[me]), (wv_hbm, wv), (wk_hbm, wk), (wq_hbm, wq)))
    ]
    for copy in loads:
        copy.start()
    for b in range(8):
        ints[b] = jnp.zeros((8, BLK), I32)
        ints[b, 0:1, :] = bits[b : b + 1, :]
        ints[b, 1:2, 0:SLOTS] = slots[b]
        ints[b, 2:3, :] = ids[b % 2 : b % 2 + 1, :]
        ints[b, 3:4, :] = jnp.broadcast_to(counts[b : b + 1, :], (1, BLK))
    loads[0].wait()
    pl.semaphore_wait(barrier, len(peers))

    def remote(src, dst, send, recv, to):
        return pltpu.make_async_remote_copy(
            src_ref=src, dst_ref=dst, send_sem=send, recv_sem=recv, device_id=to, device_id_type=MESH
        )

    sent = []

    def go(copy):
        copy.start()
        sent.append(copy)

    legs = ((3, 0, 1), (3, 1, 1), (1, 1, 3), (1, 0, 3), (2, 0, 1), (2, 1, 3))

    def half_ref(row, at, part):
        b = blk(c, at, 0) if row == 0 else blk(c, row - 1, at)
        return fbuf.at[b, pl.ds(part * BLK, BLK)]

    def leg(row, n, at):
        _, part, step = legs[n]
        to = blk(c, step, 0) if row == 0 else blk(c, 0, step)
        r = half_ref(row, at, part)
        return remote(r, r, ring_send.at[row, n], ring_recv.at[row, n], (to, z))

    def spread(row):
        for n in (0, 2, 1, 3):
            go(leg(row, n, 0))

    def arrive(row, *ns):
        for n in ns:
            leg(row, n, legs[n][0]).wait_recv()

    def forward(row):
        arrive(row, 0)
        go(leg(row, 4, 3))
        arrive(row, 2)
        go(leg(row, 5, 1))

    def share(*places):
        for i, j in places:
            b = blk(c, i, j)
            go(remote(fbuf.at[b], fbuf.at[b], sib_send.at[i, j], sib_recv.at[i, j], (sibling, z)))

    def shared(*places):
        for i, j in places:
            b = blk(1 - c, i, j)
            remote(fbuf.at[b], fbuf.at[b], sib_send.at[i, j], sib_recv.at[i, j], (sibling, z)).wait_recv()

    def project(b):
        f = fbuf[b]
        kb[b] = jnp.dot(f, wk[...], preferred_element_type=F32).astype(BF)
        v = nt(wvt[...], f).astype(BF)
        vt[b, 0] = v[:, :BLK]
        vt[b, 1] = v[:, BLK:]

    def project_many(core, *places):
        code = 0
        for i, j in reversed(places):
            code = code * 16 + 4 * i + j

        def body(e, code):
            project(blk(core, code % 16 // 4, code % 4))
            return code // 16

        lax.fori_loop(0, len(places), body, jnp.int32(code))

    spread(0)
    spread(1)
    share((0, 0))
    for dy in range(4):
        for dc in range(2):
            s = (2 * y + dy) % 4
            src = ints.at[2 * s + dc]
            slot = 2 * s + c
            if dy == 0 and dc == 0:
                local_ints = pltpu.make_async_copy(src, got.at[slot], i_recv.at[dy, dc])
                local_ints.start()
            else:
                go(
                    remote(
                        src, got.at[slot], i_send.at[dy, dc], i_recv.at[dy, dc],
                        (dst_index(x, y + dy, flip(c, dc)), z),
                    )
                )
    forward(0)
    forward(1)
    for copy in loads[1:]:
        copy.wait()
    wvt[...] = wv[...].T
    arrive(0, 1, 3)
    spread(4)
    spread(2)
    share((3, 0), (1, 0))
    arrive(0, 4, 5)
    spread(3)
    share((2, 0))
    arrive(1, 1, 3)
    share((0, 3), (0, 1))
    arrive(1, 4, 5)
    share((0, 2))
    shared((0, 0))
    project(me)
    project(sibling)
    project_many(c, (1, 0), (3, 0), (0, 1))
    shared((1, 0), (3, 0), (0, 1), (0, 3), (2, 0), (0, 2))

    yy = (z - y + 4) % 4

    def plane_rows(cc):
        return fbuf.at[dst_index(x, yy, cc), pl.ds(pl.multiple_of(flip(c, cc) * BLK, BLK), BLK)]

    for first in range(2):
        for up, to in ((0, zup), (1, zdown)):
            cc = flip(first, up)
            go(remote(plane_rows(cc), dq.at[z, cc], z_send.at[up, cc], z_recv.at[up, cc], (me, to)))
    own_copies = [pltpu.make_async_copy(plane_rows(cc), dq.at[z, cc], z_recv.at[3, cc]) for cc in range(2)]
    for copy in own_copies:
        copy.start()

    forward(4)
    forward(2)
    project_many(c, (0, 3), (2, 0), (0, 2))
    wqt[...] = wq[...].T
    wkt[...] = wk[...].T
    arrive(4, 1, 3)
    share((3, 3), (3, 1))
    arrive(2, 1, 3)
    share((1, 3), (1, 1))
    project_many(1 - c, (1, 0), (3, 0))
    forward(3)

    def z_leg(up, cc, frm):
        return remote(dq.at[frm, cc], dq.at[frm, cc], z_send.at[up, cc], z_recv.at[up, cc], (me, zup))

    z_leg(0, 0, zdown).wait_recv()
    go(remote(dq.at[zdown, 0], dq.at[zdown, 0], z_send.at[2, 0], z_recv.at[2, 0], (me, zup)))
    z_leg(1, 1, zup).wait_recv()
    go(remote(dq.at[zup, 1], dq.at[zup, 1], z_send.at[2, 1], z_recv.at[2, 1], (me, zdown)))
    project_many(1 - c, (0, 1), (0, 3), (2, 0), (0, 2))
    project_many(c, (1, 1), (1, 3), (3, 1), (3, 3))
    for copy in own_copies:
        copy.wait()

    def query(s, cc):
        q = nt(wqt[...], dq[s, cc]).astype(BF)
        q_out[2 * s + cc] = q * 0.125

    def queries(e, carry):
        query((z + 3 + e // 2) % 4, e % 2)
        return carry

    z_leg(0, 1, zdown).wait_recv()
    z_leg(1, 0, zup).wait_recv()
    arrive(4, 4, 5)
    share((3, 2))
    arrive(2, 4, 5)
    share((1, 2))
    shared((1, 1), (1, 3), (3, 1), (3, 3))
    project_many(1 - c, (1, 1), (1, 3), (3, 1), (3, 3))
    lax.fori_loop(0, 6, queries, 0)
    for cc in range(2):
        f = dq[z, cc]
        dq_out[cc] = f
        k = nt(wkt[...], f).astype(BF).astype(F32)
        q = q_out[2 * z + cc].astype(F32)
        prod = k * q
        self_score[cc] = jnp.concatenate(
            [jnp.sum(prod[h * HD : (h + 1) * HD], axis=0, keepdims=True) for h in range(HEADS)], axis=0
        )
        self_value[cc] = nt(wvt[...], f).astype(BF)
    local_ints.wait()
    for dy in range(4):
        for dc in range(2):
            if dy or dc:
                slot = 2 * ((2 * y + 4 - dy) % 4) + flip(c, dc)
                remote(
                    got.at[slot], got.at[slot], i_send.at[dy, dc], i_recv.at[dy, dc], (sibling, z)
                ).wait_recv()
    ints_out[...] = got[...]
    project_many(c, (1, 2), (3, 2))
    arrive(3, 1, 3)
    share((2, 3), (2, 1))
    far = (z + 2) % 4
    for cc in range(2):
        z_leg(2, cc, far).wait_recv()
    for cc in range(2):
        query(far, cc)
    shared((1, 2), (3, 2))
    project_many(1 - c, (1, 2), (3, 2))
    project_many(c, (2, 1), (2, 3))
    arrive(3, 4, 5)
    share((2, 2))
    project_many(c, (2, 2))
    shared((2, 1), (2, 3), (2, 2))
    project_many(1 - c, (2, 1), (2, 3), (2, 2))
    for copy in sent:
        copy.wait_send()


def gather_call(*args):
    hbm = pl.BlockSpec(memory_space=pltpu.HBM)
    vm = pl.BlockSpec(memory_space=pltpu.VMEM)
    dma = pltpu.SemaphoreType.DMA
    return pl.pallas_call(
        gather_kernel,
        out_shape=(
            pltpu.VMEM((32, ROWS, WIDTH), BF),
            pltpu.VMEM((32, 2, WIDTH, BLK), BF),
            pltpu.VMEM((8, WIDTH, BLK), BF),
            jax.ShapeDtypeStruct((8, 8, BLK), I32),
            pltpu.VMEM((2, BLK, WIDTH), BF),
            pltpu.VMEM((2, HEADS, BLK), F32),
            pltpu.VMEM((2, WIDTH, BLK), BF),
        ),
        in_specs=[hbm] * 4 + [vm] * 4,
        out_specs=(vm,) * 7,
        scratch_shapes=[
            pltpu.VMEM((32, ROWS, WIDTH), BF),
            *[pltpu.VMEM((WIDTH, WIDTH), BF)] * 6,
            pltpu.VMEM((4, 2, BLK, WIDTH), BF),
            pltpu.VMEM((8, 8, BLK), I32),
            pltpu.VMEM((8, 8, BLK), I32),
            dma((5, 6)), dma((5, 6)), dma((4, 4)), dma((4, 4)),
            dma((3, 2)), dma((4, 2)), dma((4, 2)), dma((4, 2)), dma((4,)),
        ],
        compiler_params=pltpu.CompilerParams(
            collective_id=0, has_side_effects=True, vmem_limit_bytes=44 << 20
        ),
        name="gather_project",
    )(*args)


def attention_kernel(
    lists, qt, bits, self_score, self_value, kb, vt,
    acc_out, stat_out,
    et, rhs, acc, m, l, sched, sx, sy, mx, my,
):
    x, y, c, z = place()
    lane = lax.broadcasted_iota(I32, (BLK, BLK), 1)
    row = lax.broadcasted_iota(I32, (BLK, BLK), 0)
    for ph in range(15):
        et[ph] = jnp.where((row + 2 * ph) % 30 == lane, 1.0, 0.0).astype(BF)
    et[15] = jnp.where(lane == 31, 1.0, 0.0).astype(BF)

    def phase(g):
        return (4 * ((g // 2) * 8 + 2 * z + g % 2)) % 15

    def build(b, n):
        count = lists[b, 3, 0]

        def inner(t, n):
            first = lists[b, 1, 2 * t]
            live = 2 * t + 1 < count
            second = jnp.where(live, lists[b, 1, jnp.minimum(2 * t + 1, SLOTS - 1)], first)
            sched[0, n] = b
            sched[1, n] = first
            sched[2, n] = second
            sched[3, n] = phase(first)
            sched[4, n] = jnp.where(live, phase(second), 15)
            return n + 1

        return lax.fori_loop(0, (count + 1) // 2, inner, n)

    steps = lax.fori_loop(0, 8, build, 0)
    for extra in range(2):
        for f in range(5):
            sched[f, steps + extra] = 15 if f >= 3 else 0
    even = 2 * ((steps + 1) // 2)

    def prepare(b, carry):
        brow = bits[b, 0:1, :]
        rr = lax.broadcasted_iota(I32, (32, BLK), 0)
        on = (jnp.broadcast_to(brow, (32, BLK)) >> rr) & 1
        g = jnp.where(on == 1, 0.0, OUT_MASK)
        g = jnp.where(rr < 30, g, jnp.where(rr == 31, OUT_MASK, 0.0)).astype(BF)
        gg = jnp.concatenate([g, g], 1)
        z64 = jnp.zeros((HD, BLK), BF)
        for p in range(4):
            rhs[b, p, 0:64, 0:128] = qt[b, 128 * p : 128 * p + 64, :]
            rhs[b, p, 0:64, 128:256] = z64
            rhs[b, p, 64:128, 0:128] = z64
            rhs[b, p, 64:128, 128:256] = qt[b, 128 * p + 64 : 128 * p + 128, :]
            rhs[b, p, 128:160, :] = gg
            rhs[b, p, 160:256, :] = jnp.zeros((96, 256), BF)
        m[b] = jnp.full((HEADS, BLK), FLOOR, F32)
        l[b] = jnp.zeros((HEADS, BLK), F32)
        acc[b] = jnp.zeros((WIDTH, BLK), F32)
        return carry

    lax.fori_loop(0, 8, prepare, 0)
    for cc in range(2):
        b = 2 * z + cc
        start = (dst_index(x, z - y + 4, cc) * 8 + 2 * z + flip(c, cc)) * BLK
        lanes = lax.broadcasted_iota(I32, (1, BLK), 1)
        on = (bits[b, 0:1, :] >> ((start + lanes) % 30)) & 1
        extra = jnp.broadcast_to(on, (HEADS, BLK)) == 0
        m[b] = jnp.where(extra, self_score[cc], FLOOR)
        l[b] = jnp.where(extra, 1.0, 0.0)
        acc[b] = jnp.where(
            jnp.broadcast_to(on, (WIDTH, BLK)) == 0, self_value[cc].astype(F32), 0.0
        )

    def scores(i, out, tops, p):
        e0, e1, b = et[sched[3, i]], et[sched[4, i]], sched[0, i]
        cols = slice(128 * p, 128 * p + 128)
        k0, k1 = kb[sched[1, i], :, cols], kb[sched[2, i], :, cols]
        lhs = jnp.concatenate([jnp.concatenate([k0, e0], 1), jnp.concatenate([k1, e1], 1)], 0)
        s = jnp.dot(lhs, rhs[b, p], preferred_element_type=F32)
        out[p] = s
        top = jnp.max(s.reshape(32, 8, 256), axis=0)
        tops[2 * p] = top[:, :128]
        tops[2 * p + 1] = top[:, 128:]

    def head(i, cur, tops, h):
        b = sched[0, i]
        p, side = h // 2, h % 2
        old = m[b, h : h + 1, :]
        top = jnp.maximum(old, jnp.max(tops[h], axis=0, keepdims=True))
        factor = jnp.exp(old - top)
        w = jnp.exp(cur[p, :, 128 * side : 128 * side + 128] - top)
        m[b, h : h + 1, :] = top
        l[b, h : h + 1, :] = l[b, h : h + 1, :] * factor + jnp.sum(w, axis=0, keepdims=True)
        rows = slice(64 * h, 64 * h + 64)
        v = jnp.concatenate([vt[sched[1, i], rows, :], vt[sched[2, i], rows, :]], 1)
        o = jnp.dot(v, w.astype(BF), preferred_element_type=F32)
        acc[b, rows, :] = acc[b, rows, :] * factor + o

    def step(i, cur, tops, nxt, next_tops):
        for p in range(4):
            scores(i + 1, nxt, next_tops, p)
            head(i, cur, tops, 2 * p)
            head(i, cur, tops, 2 * p + 1)

    for p in range(4):
        scores(0, sx, mx, p)

    def body(j, carry):
        step(2 * j, sx, mx, sy, my)
        step(2 * j + 1, sy, my, sx, mx)
        return carry

    lax.fori_loop(0, even // 2, body, 0)
    acc_out[...] = acc[...].astype(BF)
    stat_out[:, 0:8, :] = m[...]
    stat_out[:, 8:16, :] = l[...]


def attention_call(ints, qt, self_score, self_value, kb, vt):
    vm = pl.BlockSpec(memory_space=pltpu.VMEM)
    sm = pl.BlockSpec(memory_space=pltpu.SMEM)
    return pl.pallas_call(
        attention_kernel,
        out_shape=(
            pltpu.VMEM((8, WIDTH, BLK), BF),
            pltpu.VMEM((8, 16, BLK), F32),
        ),
        in_specs=[sm, vm, vm, vm, vm, vm, vm],
        out_specs=(vm, vm),
        scratch_shapes=[
            pltpu.VMEM((16, BLK, BLK), BF),
            pltpu.VMEM((8, 4, 256, 256), BF),
            pltpu.VMEM((8, WIDTH, BLK), F32),
            pltpu.VMEM((8, HEADS, BLK), F32),
            pltpu.VMEM((8, HEADS, BLK), F32),
            pltpu.SMEM((5, 136), I32),
            pltpu.VMEM((4, 256, 256), F32),
            pltpu.VMEM((4, 256, 256), F32),
            pltpu.VMEM((8, 8, BLK), F32),
            pltpu.VMEM((8, 8, BLK), F32),
        ],
        compiler_params=pltpu.CompilerParams(vmem_limit_bytes=24 << 20),
        name="block_attention",
    )(ints, qt, ints, self_score, self_value, kb, vt)


def merge_kernel(
    acc, stat, dq, ids, w_out,
    updated_out, pooled_out,
    acc_got, stat_got, acc_way, stat_way, made, mine, part, ring_part, total, all_part,
    a_send, a_recv, s_send, s_recv, u_send, u_recv, r_send, r_recv, g_send, g_recv,
):
    x, y, c, z = place()
    me = dst_index(x, y, c)
    ring = []
    for dy in range(4):
        for dc in range(2):
            if dy or dc:
                ring.append((dy, dc, (dst_index(x, y + dy, flip(c, dc)), z)))
    far = []
    for dx in range(4):
        for dz in range(4):
            if dx or dz:
                far.append((dx, dz, (dst_index(x + dx, y, c), (z + dz) % 4)))
    barrier = pltpu.get_barrier_semaphore()
    for _, _, peer in ring + far:
        pl.semaphore_signal(barrier, inc=1, device_id=peer, device_id_type=MESH)
    pl.semaphore_wait(barrier, len(ring) + len(far))

    def remote(src, dst, send, recv, to):
        return pltpu.make_async_remote_copy(
            src_ref=src, dst_ref=dst, send_sem=send, recv_sem=recv, device_id=to, device_id_type=MESH
        )

    sent = []

    def go(copy):
        copy.start()
        sent.append(copy)

    zup, zdown, zfar = (z + 1) % 4, (z + 3) % 4, (z + 2) % 4

    def ship(slot, acc_ref, stat_ref, to):
        go(remote(acc_ref, acc_got.at[slot], a_send.at[slot], a_recv.at[slot], (me, to)))
        go(remote(stat_ref, stat_got.at[slot], s_send.at[slot], s_recv.at[slot], (me, to)))

    def landed(slot):
        remote(acc.at[0], acc_got.at[slot], a_send.at[slot], a_recv.at[slot], (me, zup)).wait_recv()
        remote(stat.at[0], stat_got.at[slot], s_send.at[slot], s_recv.at[slot], (me, zup)).wait_recv()

    for side, to in ((0, zup), (1, zdown)):
        ship(side, acc.at[2 * zfar + side], stat.at[2 * zfar + side], to)
    for side, to in ((0, zup), (1, zdown)):
        b = 2 * to + 1 - side
        ship(2 + side, acc.at[b], stat.at[b], to)

    def weigh(stats):
        top = stats[0][0:8]
        for s in stats[1:]:
            top = jnp.maximum(top, s[0:8])
        factors = [jnp.exp(s[0:8] - top) for s in stats]
        return top, factors, sum(f * s[8:16] for f, s in zip(factors, stats))

    for side, to in ((0, zup), (1, zdown)):
        b = 2 * to + side
        landed(side)
        top, factors, whole = weigh([stat[b], stat_got[side]])
        stat_way[side, 0:8] = top
        stat_way[side, 8:16] = whole
        for h in range(HEADS):
            rows = slice(64 * h, 64 * h + 64)
            acc_way[side, rows] = (
                acc[b, rows, :].astype(F32) * factors[0][h : h + 1, :]
                + acc_got[side, rows, :].astype(F32) * factors[1][h : h + 1, :]
            ).astype(BF)
        ship(4 + side, acc_way.at[side], stat_way.at[side], to)
    for side in range(2):
        landed(2 + side)
    yy = (z - y + 4) % 4
    for cc in range(2):
        b = 2 * z + cc
        landed(4 + cc)
        slots = (3 - cc, 4 + cc)
        _, factors, whole = weigh([stat[b]] + [stat_got[k] for k in slots])
        inv = 1.0 / whole
        factors = [f * inv for f in factors]
        pieces = []
        for h in range(HEADS):
            rows = slice(64 * h, 64 * h + 64)
            o = acc[b, rows, :].astype(F32) * factors[0][h : h + 1, :]
            for n, k in enumerate(slots):
                o = o + acc_got[k, rows, :].astype(F32) * factors[n + 1][h : h + 1, :]
            pieces.append(o)
        att = jnp.concatenate(pieces, 0).T.astype(BF)
        mixed = jnp.dot(att, w_out[...], preferred_element_type=F32)
        new = (dq[cc].astype(F32) + mixed).astype(BF)
        made[cc] = new
        gid = ids[b, 2:3, :]
        graph = lax.broadcasted_iota(I32, (8, BLK), 0) % 4
        member = jnp.where(jnp.broadcast_to(gid, (8, BLK)) == graph, 1.0, 0.0)
        sums = jnp.dot(member.astype(BF), new, preferred_element_type=F32)
        low = lax.broadcasted_iota(I32, (8, 256), 0) < 4
        counts = jnp.broadcast_to(jnp.sum(member, axis=1, keepdims=True), (8, BLK))
        both = jnp.concatenate([jnp.where(low, sums[:, :256], sums[:, 256:]), counts], 1)
        part[...] = both if cc == 0 else part[...] + both
    for cc in range(2):
        own = jnp.logical_and(yy == y, c == cc)
        half = flip(c, cc)
        copy = remote(made.at[cc], mine.at[half], u_send.at[cc], u_recv.at[half], (dst_index(x, yy, cc), z))
        local = pltpu.make_async_copy(made.at[cc], mine.at[half], u_recv.at[half])
        pl.when(jnp.logical_not(own))(copy.start)
        pl.when(own)(local.start)
    for dy, dc, to in ring:
        k = 2 * dy + dc
        go(remote(part, ring_part.at[k], r_send.at[k], r_recv.at[k], to))
    whole = part[...]
    for dy, dc, to in ring:
        k = 2 * dy + dc
        remote(part, ring_part.at[k], r_send.at[k], r_recv.at[k], to).wait_recv()
        whole = whole + ring_part[k]
    total[...] = whole
    for dx, dz, to in far:
        k = 4 * dx + dz
        go(remote(total, all_part.at[k], g_send.at[k], g_recv.at[k], to))
    for half in range(2):
        pltpu.make_async_copy(made.at[half], mine.at[half], u_recv.at[half]).wait()
    updated_out[0:BLK, :] = mine[0]
    updated_out[BLK:ROWS, :] = mine[1]
    for dx, dz, to in far:
        k = 4 * dx + dz
        remote(total, all_part.at[k], g_send.at[k], g_recv.at[k], to).wait_recv()
        whole = whole + all_part[k]
    scale = 1.0 / jnp.sqrt(jnp.concatenate([whole[0:4, 256:]] * 2, 1))
    pooled_out[:, 0:256] = whole[0:4, 0:256] * scale
    pooled_out[:, 256:512] = whole[4:8, 0:256] * scale
    for cc in range(2):
        own = jnp.logical_and(yy == y, c == cc)
        copy = remote(
            made.at[cc], mine.at[flip(c, cc)], u_send.at[cc], u_recv.at[flip(c, cc)],
            (dst_index(x, yy, cc), z),
        )
        pl.when(jnp.logical_not(own))(copy.wait_send)
    for copy in sent:
        copy.wait_send()


def merge_call(acc, stat, dq, ids, w_out):
    vm = pl.BlockSpec(memory_space=pltpu.VMEM)
    dma = pltpu.SemaphoreType.DMA
    return pl.pallas_call(
        merge_kernel,
        out_shape=(
            jax.ShapeDtypeStruct((ROWS, WIDTH), BF),
            jax.ShapeDtypeStruct((4, WIDTH), F32),
        ),
        in_specs=[vm] * 5,
        out_specs=(vm, vm),
        scratch_shapes=[
            pltpu.VMEM((6, WIDTH, BLK), BF),
            pltpu.VMEM((6, 16, BLK), F32),
            pltpu.VMEM((2, WIDTH, BLK), BF),
            pltpu.VMEM((2, 16, BLK), F32),
            pltpu.VMEM((2, BLK, WIDTH), BF),
            pltpu.VMEM((2, BLK, WIDTH), BF),
            pltpu.VMEM((8, 256 + BLK), F32),
            pltpu.VMEM((8, 8, 256 + BLK), F32),
            pltpu.VMEM((8, 256 + BLK), F32),
            pltpu.VMEM((16, 8, 256 + BLK), F32),
            dma((6,)), dma((6,)), dma((6,)), dma((6,)), dma((2,)), dma((2,)),
            dma((8,)), dma((8,)), dma((16,)), dma((16,)),
        ],
        compiler_params=pltpu.CompilerParams(
            collective_id=1, has_side_effects=True, vmem_limit_bytes=16 << 20
        ),
        name="merge_project_pool",
    )(acc, stat, dq, ids, w_out)


def shards(features, w_query, w_key, w_value, w_out, node_bits, block_src, block_count, graph_ids):
    kb, vt, qt, got, dq, self_score, self_value = gather_call(
        features, w_query, w_key, w_value,
        node_bits.reshape(8, BLK), block_src, block_count, graph_ids.reshape(2, BLK),
    )
    acc, stat = attention_call(
        got, qt, self_score, self_value, kb.reshape(64, BLK, WIDTH), vt.reshape(64, WIDTH, BLK)
    )
    return merge_call(acc, stat, dq, got, w_out)


def solution(mesh):
    placed = (
        P(("dst", "src"), None),
        P(),
        P(),
        P(),
        P(),
        P("dst"),
        P("dst", "src", None),
        P("dst", "src"),
        P(("dst", "src")),
    )
    return jax.shard_map(
        shards,
        mesh=mesh,
        in_specs=placed,
        out_specs=(P(("dst", "src"), None), P()),
        check_vma=False,
    )
```

```python
import functools

import jax
import jax.numpy as jnp
from jax import lax
from jax.experimental import pallas as pl
from jax.experimental.pallas import tpu as pltpu
from jax.sharding import PartitionSpec as P

MESH = pl.DeviceIdType.MESH
BF, F32, I32 = jnp.bfloat16, jnp.float32, jnp.int32
WIDTH, HEADS, HD, BLK, ROWS = 512, 8, 64, 128, 256
SLOTS = 32
OUT_MASK = -3e38
FLOOR = -1e30
RING = 4


def place():
    d = lax.axis_index("dst")
    return d // 8, (d // 2) % 4, d % 2, lax.axis_index("src")


def dst_index(x, y, core):
    return (x % 4) * 8 + (y % 4) * 2 + core


def flip(a, b):
    return a + b - 2 * a * b


def nt(a, b):
    return lax.dot_general(a, b, (((1,), (1,)), ((), ())), preferred_element_type=F32)


def gather_kernel(
    feat, wq_hbm, wk_hbm, wv_hbm, bits, slots, counts, ids,
    kb, vt, q_out, ints_out, dq_out, self_score, self_value,
    fbuf, wq, wk, wv, wqt, wkt, wvt, dq, ints, got,
    ring_send, ring_recv, sib_send, sib_recv, z_send, z_recv, i_send, i_recv, x_send, x_recv, in_sem,
):
    x, y, c, z = place()
    me = dst_index(x, y, c)
    sibling = dst_index(x, y, 1 - c)

    def blk(core, i, j):
        return dst_index(x + (1 - core) * i + core * j, y + core * i + (1 - core) * j, core)

    zup, zdown = (z + 1) % 4, (z + 3) % 4
    peers = [(dst_index(x + 1, y, c), z), (dst_index(x + 3, y, c), z), (me, zup), (me, zdown)]
    for dy in range(4):
        for dc in range(2):
            if dy or dc:
                peers.append((dst_index(x, y + dy, flip(c, dc)), z))
    barrier = pltpu.get_barrier_semaphore()
    for peer in peers:
        pl.semaphore_signal(barrier, inc=1, device_id=peer, device_id_type=MESH)
    loads = [
        pltpu.make_async_copy(src, dst, in_sem.at[n])
        for n, (src, dst) in enumerate(((feat, fbuf.at[me]), (wv_hbm, wv), (wk_hbm, wk), (wq_hbm, wq)))
    ]
    for copy in loads:
        copy.start()
    for b in range(8):
        ints[b] = jnp.zeros((8, BLK), I32)
        ints[b, 0:1, :] = bits[b : b + 1, :]
        ints[b, 1:2, 0:SLOTS] = slots[b]
        ints[b, 2:3, :] = ids[b % 2 : b % 2 + 1, :]
        ints[b, 3:4, :] = jnp.broadcast_to(counts[0:1, b : b + 1], (1, BLK))
    loads[0].wait()
    pl.semaphore_wait(barrier, len(peers))

    def remote(src, dst, send, recv, to):
        return pltpu.make_async_remote_copy(
            src_ref=src, dst_ref=dst, send_sem=send, recv_sem=recv, device_id=to, device_id_type=MESH
        )

    sent = []

    def go(copy):
        copy.start()
        sent.append(copy)

    legs = ((3, 0, 1), (3, 1, 1), (1, 1, 3), (1, 0, 3), (2, 0, 1), (2, 1, 3))

    def half_ref(row, at, part):
        b = blk(c, at, 0) if row == 0 else blk(c, row - 1, at)
        return fbuf.at[b, pl.ds(part * BLK, BLK)]

    def leg(row, n, at):
        _, part, step = legs[n]
        to = blk(c, step, 0) if row == 0 else blk(c, 0, step)
        r = half_ref(row, at, part)
        return remote(r, r, ring_send.at[row, n], ring_recv.at[row, n], (to, z))

    def spread(row):
        for n in (0, 2, 1, 3):
            go(leg(row, n, 0))

    def arrive(row, *ns):
        for n in ns:
            leg(row, n, legs[n][0]).wait_recv()

    def forward(row):
        arrive(row, 0)
        go(leg(row, 4, 3))
        arrive(row, 2)
        go(leg(row, 5, 1))

    def handed(core, i, j):
        b = blk(core, i, j)
        return [
            remote(r.at[b], r.at[b], sib_send.at[i, j, n], sib_recv.at[i, j, n], (sibling, z))
            for n, r in enumerate((kb, vt))
        ]

    def project(i, j):
        b = blk(c, i, j)
        keys, values = handed(c, i, j)
        f = fbuf[b]
        kb[b] = jnp.dot(f, wk[...], preferred_element_type=F32).astype(BF)
        keys.start()
        v = nt(wvt[...], f).astype(BF)
        vt[b, 0] = v[:, :BLK]
        vt[b, 1] = v[:, BLK:]
        values.start()

    def project_many(*places):
        code = 0
        for i, j in reversed(places):
            code = code * 16 + 4 * i + j

        def body(e, code):
            project(code % 16 // 4, code % 4)
            return code // 16

        lax.fori_loop(0, len(places), body, jnp.int32(code))

    spread(0)
    spread(1)
    for dy in range(4):
        for dc in range(2):
            s = (2 * y + dy) % 4
            src = ints.at[2 * s + dc]
            slot = 2 * s + c
            if dy == 0 and dc == 0:
                local_ints = pltpu.make_async_copy(src, got.at[slot], i_recv.at[dy, dc])
                local_ints.start()
            else:
                go(
                    remote(
                        src, got.at[slot], i_send.at[dy, dc], i_recv.at[dy, dc],
                        (dst_index(x, y + dy, flip(c, dc)), z),
                    )
                )
    forward(0)
    forward(1)
    for copy in loads[1:]:
        copy.wait()
    wvt[...] = wv[...].T
    arrive(0, 1, 3)
    spread(4)
    spread(2)
    arrive(0, 4, 5)
    spread(3)
    arrive(1, 1, 3)
    arrive(1, 4, 5)

    yy = (z - y + 4) % 4

    def plane_rows(half):
        return fbuf.at[dst_index(x, yy, c), pl.ds(half * BLK, BLK)]

    cross = remote(plane_rows(1), dq.at[z, c], x_send.at[0], x_recv.at[0], (sibling, z))
    go(cross)
    own_copy = pltpu.make_async_copy(plane_rows(0), dq.at[z, c], in_sem.at[4])
    own_copy.start()
    for up, to in ((0, zup), (1, zdown)):
        go(remote(plane_rows(0), dq.at[z, c], z_send.at[up, c], z_recv.at[up, c], (me, to)))
    project_many((0, 0), (1, 0))
    remote(dq.at[z, 1 - c], dq.at[z, 1 - c], x_send.at[0], x_recv.at[0], (sibling, z)).wait_recv()
    for up, to in ((0, zup), (1, zdown)):
        go(remote(dq.at[z, 1 - c], dq.at[z, 1 - c], z_send.at[up, 1 - c], z_recv.at[up, 1 - c], (me, to)))
    project_many((3, 0), (0, 1))
    forward(4)
    forward(2)
    wqt[...] = wq[...].T
    wkt[...] = wk[...].T
    project_many((0, 3), (2, 0), (0, 2))
    forward(3)
    arrive(4, 1, 3)
    arrive(2, 1, 3)

    def z_leg(up, cc, frm):
        return remote(dq.at[frm, cc], dq.at[frm, cc], z_send.at[up, cc], z_recv.at[up, cc], (me, zup))

    z_leg(0, 0, zdown).wait_recv()
    go(remote(dq.at[zdown, 0], dq.at[zdown, 0], z_send.at[2, 0], z_recv.at[2, 0], (me, zup)))
    z_leg(1, 1, zup).wait_recv()
    go(remote(dq.at[zup, 1], dq.at[zup, 1], z_send.at[2, 1], z_recv.at[2, 1], (me, zdown)))
    project_many((1, 1), (1, 3), (3, 1), (3, 3))
    own_copy.wait()

    def query(s, cc):
        q = nt(wqt[...], dq[s, cc]).astype(BF)
        q_out[2 * s + cc] = q * 0.125

    def queries(e, carry):
        query((z + 3 + e // 2) % 4, e % 2)
        return carry

    z_leg(0, 1, zdown).wait_recv()
    z_leg(1, 0, zup).wait_recv()
    lax.fori_loop(0, 6, queries, 0)
    for cc in range(2):
        f = dq[z, cc]
        dq_out[cc] = f
        k = nt(wkt[...], f).astype(BF).astype(F32)
        q = q_out[2 * z + cc].astype(F32)
        prod = k * q
        self_score[cc] = jnp.concatenate(
            [jnp.sum(prod[h * HD : (h + 1) * HD], axis=0, keepdims=True) for h in range(HEADS)], axis=0
        )
        self_value[cc] = nt(wvt[...], f).astype(BF)
    local_ints.wait()
    for dy in range(4):
        for dc in range(2):
            if dy or dc:
                slot = 2 * ((2 * y + 4 - dy) % 4) + flip(c, dc)
                remote(
                    got.at[slot], got.at[slot], i_send.at[dy, dc], i_recv.at[dy, dc], (sibling, z)
                ).wait_recv()
    ints_out[...] = got[...]
    arrive(4, 4, 5)
    arrive(2, 4, 5)
    project_many((3, 2), (1, 2))
    arrive(3, 1, 3)
    project_many((2, 1), (2, 3))
    far = (z + 2) % 4
    for cc in range(2):
        z_leg(2, cc, far).wait_recv()
    for cc in range(2):
        query(far, cc)
    arrive(3, 4, 5)
    project(2, 2)
    for i in range(4):
        for j in range(4):
            for copy in handed(1 - c, i, j):
                copy.wait_recv()
            for copy in handed(c, i, j):
                copy.wait_send()
    for copy in sent:
        copy.wait_send()


def gather_call(*args):
    hbm = pl.BlockSpec(memory_space=pltpu.HBM)
    vm = pl.BlockSpec(memory_space=pltpu.VMEM)
    dma = pltpu.SemaphoreType.DMA
    return pl.pallas_call(
        gather_kernel,
        out_shape=(
            pltpu.VMEM((32, ROWS, WIDTH), BF),
            pltpu.VMEM((32, 2, WIDTH, BLK), BF),
            pltpu.VMEM((8, WIDTH, BLK), BF),
            pltpu.VMEM((8, 8, BLK), I32),
            pltpu.VMEM((2, BLK, WIDTH), BF),
            pltpu.VMEM((2, HEADS, BLK), F32),
            pltpu.VMEM((2, WIDTH, BLK), BF),
        ),
        in_specs=[hbm] * 4 + [vm] * 4,
        out_specs=(vm,) * 7,
        scratch_shapes=[
            pltpu.VMEM((32, ROWS, WIDTH), BF),
            *[pltpu.VMEM((WIDTH, WIDTH), BF)] * 6,
            pltpu.VMEM((4, 2, BLK, WIDTH), BF),
            pltpu.VMEM((8, 8, BLK), I32),
            pltpu.VMEM((8, 8, BLK), I32),
            dma((5, 6)), dma((5, 6)), dma((4, 4, 2)), dma((4, 4, 2)),
            dma((3, 2)), dma((3, 2)), dma((4, 2)), dma((4, 2)), dma((1,)), dma((1,)), dma((5,)),
        ],
        compiler_params=pltpu.CompilerParams(
            collective_id=0, has_side_effects=True, vmem_limit_bytes=44 << 20
        ),
        name="gather_project",
    )(*args)


def attention_kernel(
    qt, bits, self_score, self_value, kb, vt,
    acc_out, stat_out,
    lists, list_sem, et, rhs, acc, m, l, sched, sx, sy, mx, my,
):
    x, y, c, z = place()
    fetch = pltpu.make_async_copy(bits, lists, list_sem)
    fetch.start()
    lane = lax.broadcasted_iota(I32, (BLK, BLK), 1)
    row = lax.broadcasted_iota(I32, (BLK, BLK), 0)
    for ph in range(15):
        et[ph] = jnp.where((row + 2 * ph) % 30 == lane, 1.0, 0.0).astype(BF)
    et[15] = jnp.where(lane == 31, 1.0, 0.0).astype(BF)

    def phase(g):
        return (4 * ((g // 2) * 8 + 2 * z + g % 2)) % 15

    def build(b, n):
        count = lists[b, 3, 0]

        def inner(t, n):
            first = lists[b, 1, 2 * t]
            live = 2 * t + 1 < count
            second = jnp.where(live, lists[b, 1, jnp.minimum(2 * t + 1, SLOTS - 1)], first)
            sched[0, n] = b
            sched[1, n] = first
            sched[2, n] = second
            sched[3, n] = phase(first)
            sched[4, n] = jnp.where(live, phase(second), 15)
            return n + 1

        return lax.fori_loop(0, (count + 1) // 2, inner, n)

    fetch.wait()
    steps = lax.fori_loop(0, 8, build, 0)
    for extra in range(2):
        for f in range(5):
            sched[f, steps + extra] = 15 if f >= 3 else 0
    even = 2 * ((steps + 1) // 2)

    def prepare(b, carry):
        brow = bits[b, 0:1, :]
        rr = lax.broadcasted_iota(I32, (32, BLK), 0)
        on = (jnp.broadcast_to(brow, (32, BLK)) >> rr) & 1
        g = jnp.where(on == 1, 0.0, OUT_MASK)
        g = jnp.where(rr < 30, g, jnp.where(rr == 31, OUT_MASK, 0.0)).astype(BF)
        gg = jnp.concatenate([g, g], 1)
        z64 = jnp.zeros((HD, BLK), BF)
        for p in range(4):
            rhs[b, p, 0:64, 0:128] = qt[b, 128 * p : 128 * p + 64, :]
            rhs[b, p, 0:64, 128:256] = z64
            rhs[b, p, 64:128, 0:128] = z64
            rhs[b, p, 64:128, 128:256] = qt[b, 128 * p + 64 : 128 * p + 128, :]
            rhs[b, p, 128:160, :] = gg
            rhs[b, p, 160:256, :] = jnp.zeros((96, 256), BF)
        m[b] = jnp.full((HEADS, BLK), FLOOR, F32)
        l[b] = jnp.zeros((HEADS, BLK), F32)
        acc[b] = jnp.zeros((WIDTH, BLK), F32)
        return carry

    lax.fori_loop(0, 8, prepare, 0)
    for cc in range(2):
        b = 2 * z + cc
        start = (dst_index(x, z - y + 4, cc) * 8 + 2 * z + flip(c, cc)) * BLK
        lanes = lax.broadcasted_iota(I32, (1, BLK), 1)
        on = (bits[b, 0:1, :] >> ((start + lanes) % 30)) & 1
        extra = jnp.broadcast_to(on, (HEADS, BLK)) == 0
        m[b] = jnp.where(extra, self_score[cc], FLOOR)
        l[b] = jnp.where(extra, 1.0, 0.0)
        acc[b] = jnp.where(
            jnp.broadcast_to(on, (WIDTH, BLK)) == 0, self_value[cc].astype(F32), 0.0
        )

    def scores(i, out, tops, p):
        e0, e1, b = et[sched[3, i]], et[sched[4, i]], sched[0, i]
        cols = slice(128 * p, 128 * p + 128)
        k0, k1 = kb[sched[1, i], :, cols], kb[sched[2, i], :, cols]
        lhs = jnp.concatenate([jnp.concatenate([k0, e0], 1), jnp.concatenate([k1, e1], 1)], 0)
        s = jnp.dot(lhs, rhs[b, p], preferred_element_type=F32)
        out[p] = s
        top = jnp.max(s.reshape(32, 8, 256), axis=0)
        tops[2 * p] = top[:, :128]
        tops[2 * p + 1] = top[:, 128:]

    def head(i, cur, tops, h):
        b = sched[0, i]
        p, side = h // 2, h % 2
        old = m[b, h : h + 1, :]
        top = jnp.maximum(old, jnp.max(tops[h], axis=0, keepdims=True))
        factor = jnp.exp(old - top)
        w = jnp.exp(cur[p, :, 128 * side : 128 * side + 128] - top)
        m[b, h : h + 1, :] = top
        l[b, h : h + 1, :] = l[b, h : h + 1, :] * factor + jnp.sum(w, axis=0, keepdims=True)
        rows = slice(64 * h, 64 * h + 64)
        v = jnp.concatenate([vt[sched[1, i], rows, :], vt[sched[2, i], rows, :]], 1)
        o = jnp.dot(v, w.astype(BF), preferred_element_type=F32)
        acc[b, rows, :] = acc[b, rows, :] * factor + o

    def step(i, cur, tops, nxt, next_tops):
        for p in range(4):
            scores(i + 1, nxt, next_tops, p)
            head(i, cur, tops, 2 * p)
            head(i, cur, tops, 2 * p + 1)

    for p in range(4):
        scores(0, sx, mx, p)

    def body(j, carry):
        step(2 * j, sx, mx, sy, my)
        step(2 * j + 1, sy, my, sx, mx)
        return carry

    lax.fori_loop(0, even // 2, body, 0)
    acc_out[...] = acc[...].astype(BF)
    stat_out[:, 0:8, :] = m[...]
    stat_out[:, 8:16, :] = l[...]


def attention_call(ints, qt, self_score, self_value, kb, vt):
    vm = pl.BlockSpec(memory_space=pltpu.VMEM)
    return pl.pallas_call(
        attention_kernel,
        out_shape=(
            pltpu.VMEM((8, WIDTH, BLK), BF),
            pltpu.VMEM((8, 16, BLK), F32),
        ),
        in_specs=[vm] * 6,
        out_specs=(vm, vm),
        scratch_shapes=[
            pltpu.SMEM((8, 8, BLK), I32),
            pltpu.SemaphoreType.DMA,
            pltpu.VMEM((16, BLK, BLK), BF),
            pltpu.VMEM((8, 4, 256, 256), BF),
            pltpu.VMEM((8, WIDTH, BLK), F32),
            pltpu.VMEM((8, HEADS, BLK), F32),
            pltpu.VMEM((8, HEADS, BLK), F32),
            pltpu.SMEM((5, 136), I32),
            pltpu.VMEM((4, 256, 256), F32),
            pltpu.VMEM((4, 256, 256), F32),
            pltpu.VMEM((8, 8, BLK), F32),
            pltpu.VMEM((8, 8, BLK), F32),
        ],
        compiler_params=pltpu.CompilerParams(vmem_limit_bytes=24 << 20),
        name="block_attention",
    )(qt, ints, self_score, self_value, kb, vt)


def merge_kernel(
    acc, stat, dq, ids, w_out,
    updated_out, pooled_out,
    acc_got, stat_got, acc_way, stat_way, made, mine, part, ring_part, total, all_part,
    a_send, a_recv, s_send, s_recv, u_send, u_recv, r_send, r_recv, g_send, g_recv,
):
    x, y, c, z = place()
    me = dst_index(x, y, c)
    ring = []
    for dy in range(4):
        for dc in range(2):
            if dy or dc:
                ring.append((dy, dc, (dst_index(x, y + dy, flip(c, dc)), z)))
    far = []
    for dx in range(4):
        for dz in range(4):
            if dx or dz:
                far.append((dx, dz, (dst_index(x + dx, y, c), (z + dz) % 4)))
    barrier = pltpu.get_barrier_semaphore()
    for _, _, peer in ring + far:
        pl.semaphore_signal(barrier, inc=1, device_id=peer, device_id_type=MESH)
    pl.semaphore_wait(barrier, len(ring) + len(far))

    def remote(src, dst, send, recv, to):
        return pltpu.make_async_remote_copy(
            src_ref=src, dst_ref=dst, send_sem=send, recv_sem=recv, device_id=to, device_id_type=MESH
        )

    sent = []

    def go(copy):
        copy.start()
        sent.append(copy)

    zup, zdown, zfar = (z + 1) % 4, (z + 3) % 4, (z + 2) % 4

    def ship(slot, acc_ref, stat_ref, to):
        go(remote(acc_ref, acc_got.at[slot], a_send.at[slot], a_recv.at[slot], (me, to)))
        go(remote(stat_ref, stat_got.at[slot], s_send.at[slot], s_recv.at[slot], (me, to)))

    def landed(slot):
        remote(acc.at[0], acc_got.at[slot], a_send.at[slot], a_recv.at[slot], (me, zup)).wait_recv()
        remote(stat.at[0], stat_got.at[slot], s_send.at[slot], s_recv.at[slot], (me, zup)).wait_recv()

    for side, to in ((0, zup), (1, zdown)):
        ship(side, acc.at[2 * zfar + side], stat.at[2 * zfar + side], to)
    for side, to in ((0, zup), (1, zdown)):
        b = 2 * to + 1 - side
        ship(2 + side, acc.at[b], stat.at[b], to)

    def weigh(stats):
        top = stats[0][0:8]
        for s in stats[1:]:
            top = jnp.maximum(top, s[0:8])
        factors = [jnp.exp(s[0:8] - top) for s in stats]
        return top, factors, sum(f * s[8:16] for f, s in zip(factors, stats))

    for side, to in ((0, zup), (1, zdown)):
        b = 2 * to + side
        landed(side)
        top, factors, whole = weigh([stat[b], stat_got[side]])
        stat_way[side, 0:8] = top
        stat_way[side, 8:16] = whole
        for h in range(HEADS):
            rows = slice(64 * h, 64 * h + 64)
            acc_way[side, rows] = (
                acc[b, rows, :].astype(F32) * factors[0][h : h + 1, :]
                + acc_got[side, rows, :].astype(F32) * factors[1][h : h + 1, :]
            ).astype(BF)
        ship(4 + side, acc_way.at[side], stat_way.at[side], to)
    for side in range(2):
        landed(2 + side)
    yy = (z - y + 4) % 4
    for cc in range(2):
        b = 2 * z + cc
        landed(4 + cc)
        slots = (3 - cc, 4 + cc)
        _, factors, whole = weigh([stat[b]] + [stat_got[k] for k in slots])
        inv = 1.0 / whole
        factors = [f * inv for f in factors]
        pieces = []
        for h in range(HEADS):
            rows = slice(64 * h, 64 * h + 64)
            o = acc[b, rows, :].astype(F32) * factors[0][h : h + 1, :]
            for n, k in enumerate(slots):
                o = o + acc_got[k, rows, :].astype(F32) * factors[n + 1][h : h + 1, :]
            pieces.append(o)
        att = jnp.concatenate(pieces, 0).T.astype(BF)
        mixed = jnp.dot(att, w_out[...], preferred_element_type=F32)
        new = (dq[cc].astype(F32) + mixed).astype(BF)
        made[cc] = new
        gid = ids[b, 2:3, :]
        graph = lax.broadcasted_iota(I32, (8, BLK), 0) % 4
        member = jnp.where(jnp.broadcast_to(gid, (8, BLK)) == graph, 1.0, 0.0)
        sums = jnp.dot(member.astype(BF), new, preferred_element_type=F32)
        low = lax.broadcasted_iota(I32, (8, 256), 0) < 4
        counts = jnp.broadcast_to(jnp.sum(member, axis=1, keepdims=True), (8, BLK))
        both = jnp.concatenate([jnp.where(low, sums[:, :256], sums[:, 256:]), counts], 1)
        part[...] = both if cc == 0 else part[...] + both
    for cc in range(2):
        own = jnp.logical_and(yy == y, c == cc)
        half = flip(c, cc)
        copy = remote(made.at[cc], mine.at[half], u_send.at[cc], u_recv.at[half], (dst_index(x, yy, cc), z))
        local = pltpu.make_async_copy(made.at[cc], mine.at[half], u_recv.at[half])
        pl.when(jnp.logical_not(own))(copy.start)
        pl.when(own)(local.start)
    for dy, dc, to in ring:
        k = 2 * dy + dc
        go(remote(part, ring_part.at[k], r_send.at[k], r_recv.at[k], to))
    whole = part[...]
    for dy, dc, to in ring:
        k = 2 * dy + dc
        remote(part, ring_part.at[k], r_send.at[k], r_recv.at[k], to).wait_recv()
        whole = whole + ring_part[k]
    total[...] = whole
    for dx, dz, to in far:
        k = 4 * dx + dz
        go(remote(total, all_part.at[k], g_send.at[k], g_recv.at[k], to))
    for half in range(2):
        pltpu.make_async_copy(made.at[half], mine.at[half], u_recv.at[half]).wait()
    updated_out[0:BLK, :] = mine[0]
    updated_out[BLK:ROWS, :] = mine[1]
    for dx, dz, to in far:
        k = 4 * dx + dz
        remote(total, all_part.at[k], g_send.at[k], g_recv.at[k], to).wait_recv()
        whole = whole + all_part[k]
    scale = 1.0 / jnp.sqrt(jnp.concatenate([whole[0:4, 256:]] * 2, 1))
    pooled_out[:, 0:256] = whole[0:4, 0:256] * scale
    pooled_out[:, 256:512] = whole[4:8, 0:256] * scale
    for cc in range(2):
        own = jnp.logical_and(yy == y, c == cc)
        copy = remote(
            made.at[cc], mine.at[flip(c, cc)], u_send.at[cc], u_recv.at[flip(c, cc)],
            (dst_index(x, yy, cc), z),
        )
        pl.when(jnp.logical_not(own))(copy.wait_send)
    for copy in sent:
        copy.wait_send()


def merge_call(acc, stat, dq, ids, w_out):
    vm = pl.BlockSpec(memory_space=pltpu.VMEM)
    dma = pltpu.SemaphoreType.DMA
    return pl.pallas_call(
        merge_kernel,
        out_shape=(
            jax.ShapeDtypeStruct((ROWS, WIDTH), BF),
            jax.ShapeDtypeStruct((4, WIDTH), F32),
        ),
        in_specs=[vm] * 5,
        out_specs=(vm, vm),
        scratch_shapes=[
            pltpu.VMEM((6, WIDTH, BLK), BF),
            pltpu.VMEM((6, 16, BLK), F32),
            pltpu.VMEM((2, WIDTH, BLK), BF),
            pltpu.VMEM((2, 16, BLK), F32),
            pltpu.VMEM((2, BLK, WIDTH), BF),
            pltpu.VMEM((2, BLK, WIDTH), BF),
            pltpu.VMEM((8, 256 + BLK), F32),
            pltpu.VMEM((8, 8, 256 + BLK), F32),
            pltpu.VMEM((8, 256 + BLK), F32),
            pltpu.VMEM((16, 8, 256 + BLK), F32),
            dma((6,)), dma((6,)), dma((6,)), dma((6,)), dma((2,)), dma((2,)),
            dma((8,)), dma((8,)), dma((16,)), dma((16,)),
        ],
        compiler_params=pltpu.CompilerParams(
            collective_id=1, has_side_effects=True, vmem_limit_bytes=16 << 20
        ),
        name="merge_project_pool",
    )(acc, stat, dq, ids, w_out)


def shards(features, w_query, w_key, w_value, w_out, node_bits, block_src, block_count, graph_ids):
    kb, vt, qt, got, dq, self_score, self_value = gather_call(
        features, w_query, w_key, w_value,
        node_bits.reshape(8, BLK), block_src, block_count.reshape(1, 8), graph_ids.reshape(2, BLK),
    )
    acc, stat = attention_call(
        got, qt, self_score, self_value, kb.reshape(64, BLK, WIDTH), vt.reshape(64, WIDTH, BLK)
    )
    return merge_call(acc, stat, dq, got, w_out)


def solution(mesh):
    placed = (
        P(("dst", "src"), None),
        P(),
        P(),
        P(),
        P(),
        P("dst"),
        P("dst", "src", None),
        P("dst", "src"),
        P(("dst", "src")),
    )
    return jax.shard_map(
        shards,
        mesh=mesh,
        in_specs=placed,
        out_specs=(P(("dst", "src"), None), P()),
        check_vma=False,
    )
```

```python
import functools

import jax
import jax.numpy as jnp
from jax import lax
from jax.experimental import pallas as pl
from jax.experimental.pallas import tpu as pltpu
from jax.sharding import PartitionSpec as P

MESH = pl.DeviceIdType.MESH
BF, F32, I32 = jnp.bfloat16, jnp.float32, jnp.int32
WIDTH, HEADS, HD, BLK, ROWS = 512, 8, 64, 128, 256
SLOTS = 32
OUT_MASK = -3e38
FLOOR = -1e30
RING = 4


def place():
    d = lax.axis_index("dst")
    return d // 8, (d // 2) % 4, d % 2, lax.axis_index("src")


def dst_index(x, y, core):
    return (x % 4) * 8 + (y % 4) * 2 + core


def flip(a, b):
    return a + b - 2 * a * b


def nt(a, b):
    return lax.dot_general(a, b, (((1,), (1,)), ((), ())), preferred_element_type=F32)


def gather_kernel(
    feat, wq_hbm, wk_hbm, wv_hbm, bits, slots, counts, ids,
    kb, vt, q_out, ints_out, dq_out, self_score, self_value, et,
    fbuf, wq, wk, wv, wqt, wkt, wvt, dq, ints, got,
    ring_send, ring_recv, sib_send, sib_recv, z_send, z_recv, i_send, i_recv, x_send, x_recv, in_sem,
):
    x, y, c, z = place()
    me = dst_index(x, y, c)
    sibling = dst_index(x, y, 1 - c)

    def blk(core, i, j):
        return dst_index(x + (1 - core) * i + core * j, y + core * i + (1 - core) * j, core)

    zup, zdown = (z + 1) % 4, (z + 3) % 4
    peers = [(dst_index(x + 1, y, c), z), (dst_index(x + 3, y, c), z), (me, zup), (me, zdown)]
    for dy in range(4):
        for dc in range(2):
            if dy or dc:
                peers.append((dst_index(x, y + dy, flip(c, dc)), z))
    barrier = pltpu.get_barrier_semaphore()
    for peer in peers:
        pl.semaphore_signal(barrier, inc=1, device_id=peer, device_id_type=MESH)
    loads = [
        pltpu.make_async_copy(src, dst, in_sem.at[n])
        for n, (src, dst) in enumerate(((feat, fbuf.at[me]), (wv_hbm, wv), (wk_hbm, wk), (wq_hbm, wq)))
    ]
    for copy in loads:
        copy.start()
    for b in range(8):
        ints[b] = jnp.zeros((8, BLK), I32)
        ints[b, 0:1, :] = bits[b : b + 1, :]
        ints[b, 1:2, 0:SLOTS] = slots[b]
        ints[b, 2:3, :] = ids[b % 2 : b % 2 + 1, :]
        ints[b, 3:4, :] = jnp.broadcast_to(counts[0:1, b : b + 1], (1, BLK))
    loads[0].wait()
    pl.semaphore_wait(barrier, len(peers))

    def remote(src, dst, send, recv, to):
        return pltpu.make_async_remote_copy(
            src_ref=src, dst_ref=dst, send_sem=send, recv_sem=recv, device_id=to, device_id_type=MESH
        )

    sent = []

    def go(copy):
        copy.start()
        sent.append(copy)

    legs = ((3, 0, 1), (3, 1, 1), (1, 1, 3), (1, 0, 3), (2, 0, 1), (2, 1, 3))

    def half_ref(row, at, part):
        b = blk(c, at, 0) if row == 0 else blk(c, row - 1, at)
        return fbuf.at[b, pl.ds(part * BLK, BLK)]

    def leg(row, n, at):
        _, part, step = legs[n]
        to = blk(c, step, 0) if row == 0 else blk(c, 0, step)
        r = half_ref(row, at, part)
        return remote(r, r, ring_send.at[row, n], ring_recv.at[row, n], (to, z))

    def spread(row):
        for n in (0, 2, 1, 3):
            go(leg(row, n, 0))

    def arrive(row, *ns):
        for n in ns:
            leg(row, n, legs[n][0]).wait_recv()

    def forward(row):
        arrive(row, 0)
        go(leg(row, 4, 3))
        arrive(row, 2)
        go(leg(row, 5, 1))

    def handed(core, i, j):
        b = blk(core, i, j)
        return [
            remote(r.at[b], r.at[b], sib_send.at[i, j, n], sib_recv.at[i, j, n], (sibling, z))
            for n, r in enumerate((kb, vt))
        ]

    def project(i, j):
        b = blk(c, i, j)
        keys, values = handed(c, i, j)
        f = fbuf[b]
        kb[b] = jnp.dot(f, wk[...], preferred_element_type=F32).astype(BF)
        keys.start()
        v = nt(wvt[...], f).astype(BF)
        vt[b, 0] = v[:, :BLK]
        vt[b, 1] = v[:, BLK:]
        values.start()

    def project_many(*places):
        code = 0
        for i, j in reversed(places):
            code = code * 16 + 4 * i + j

        def body(e, code):
            project(code % 16 // 4, code % 4)
            return code // 16

        lax.fori_loop(0, len(places), body, jnp.int32(code))

    spread(0)
    spread(1)
    for dy in range(4):
        for dc in range(2):
            s = (2 * y + dy) % 4
            src = ints.at[2 * s + dc]
            slot = 2 * s + c
            if dy == 0 and dc == 0:
                local_ints = pltpu.make_async_copy(src, got.at[slot], i_recv.at[dy, dc])
                local_ints.start()
            else:
                go(
                    remote(
                        src, got.at[slot], i_send.at[dy, dc], i_recv.at[dy, dc],
                        (dst_index(x, y + dy, flip(c, dc)), z),
                    )
                )
    lane = lax.broadcasted_iota(I32, (BLK, BLK), 1)
    row = lax.broadcasted_iota(I32, (BLK, BLK), 0)
    for ph in range(15):
        et[ph] = jnp.where((row + 2 * ph) % 30 == lane, 1.0, 0.0).astype(BF)
    et[15] = jnp.where(lane == 31, 1.0, 0.0).astype(BF)
    forward(0)
    forward(1)
    for copy in loads[1:]:
        copy.wait()
    wvt[...] = wv[...].T
    arrive(0, 1, 3)
    spread(4)
    spread(2)
    arrive(0, 4, 5)
    spread(3)
    arrive(1, 1, 3)
    arrive(1, 4, 5)

    yy = (z - y + 4) % 4

    def plane_rows(half):
        return fbuf.at[dst_index(x, yy, c), pl.ds(half * BLK, BLK)]

    cross = remote(plane_rows(1), dq.at[z, c], x_send.at[0], x_recv.at[0], (sibling, z))
    go(cross)
    own_copy = pltpu.make_async_copy(plane_rows(0), dq.at[z, c], in_sem.at[4])
    own_copy.start()
    for up, to in ((0, zup), (1, zdown)):
        go(remote(plane_rows(0), dq.at[z, c], z_send.at[up, c], z_recv.at[up, c], (me, to)))
    project_many((0, 0), (1, 0))
    remote(dq.at[z, 1 - c], dq.at[z, 1 - c], x_send.at[0], x_recv.at[0], (sibling, z)).wait_recv()
    for up, to in ((0, zup), (1, zdown)):
        go(remote(dq.at[z, 1 - c], dq.at[z, 1 - c], z_send.at[up, 1 - c], z_recv.at[up, 1 - c], (me, to)))
    project_many((3, 0), (0, 1))
    forward(4)
    forward(2)
    wqt[...] = wq[...].T
    wkt[...] = wk[...].T
    project_many((0, 3), (2, 0), (0, 2))
    forward(3)
    arrive(4, 1, 3)
    arrive(2, 1, 3)

    def z_leg(up, cc, frm):
        return remote(dq.at[frm, cc], dq.at[frm, cc], z_send.at[up, cc], z_recv.at[up, cc], (me, zup))

    z_leg(0, 0, zdown).wait_recv()
    go(remote(dq.at[zdown, 0], dq.at[zdown, 0], z_send.at[2, 0], z_recv.at[2, 0], (me, zup)))
    z_leg(1, 1, zup).wait_recv()
    go(remote(dq.at[zup, 1], dq.at[zup, 1], z_send.at[2, 1], z_recv.at[2, 1], (me, zdown)))
    project_many((1, 1), (1, 3), (3, 1), (3, 3))
    own_copy.wait()

    def query(s, cc):
        q = nt(wqt[...], dq[s, cc]).astype(BF)
        q_out[2 * s + cc] = q * 0.125

    def queries(e, carry):
        query((z + 3 + e // 2) % 4, e % 2)
        return carry

    z_leg(0, 1, zdown).wait_recv()
    z_leg(1, 0, zup).wait_recv()
    lax.fori_loop(0, 6, queries, 0)
    for cc in range(2):
        f = dq[z, cc]
        dq_out[cc] = f
        k = nt(wkt[...], f).astype(BF).astype(F32)
        q = q_out[2 * z + cc].astype(F32)
        prod = k * q
        self_score[cc] = jnp.concatenate(
            [jnp.sum(prod[h * HD : (h + 1) * HD], axis=0, keepdims=True) for h in range(HEADS)], axis=0
        )
        self_value[cc] = nt(wvt[...], f).astype(BF)
    local_ints.wait()
    for dy in range(4):
        for dc in range(2):
            if dy or dc:
                slot = 2 * ((2 * y + 4 - dy) % 4) + flip(c, dc)
                remote(
                    got.at[slot], got.at[slot], i_send.at[dy, dc], i_recv.at[dy, dc], (sibling, z)
                ).wait_recv()
    ints_out[...] = got[...]
    arrive(4, 4, 5)
    arrive(2, 4, 5)
    project_many((3, 2), (1, 2))
    arrive(3, 1, 3)
    project_many((2, 1), (2, 3))
    far = (z + 2) % 4
    for cc in range(2):
        z_leg(2, cc, far).wait_recv()
    for cc in range(2):
        query(far, cc)
    arrive(3, 4, 5)
    project(2, 2)
    for i in range(4):
        for j in range(4):
            for copy in handed(1 - c, i, j):
                copy.wait_recv()
            for copy in handed(c, i, j):
                copy.wait_send()
    for copy in sent:
        copy.wait_send()


def gather_call(*args):
    hbm = pl.BlockSpec(memory_space=pltpu.HBM)
    vm = pl.BlockSpec(memory_space=pltpu.VMEM)
    dma = pltpu.SemaphoreType.DMA
    return pl.pallas_call(
        gather_kernel,
        out_shape=(
            pltpu.VMEM((32, ROWS, WIDTH), BF),
            pltpu.VMEM((32, 2, WIDTH, BLK), BF),
            pltpu.VMEM((8, WIDTH, BLK), BF),
            pltpu.VMEM((8, 8, BLK), I32),
            pltpu.VMEM((2, BLK, WIDTH), BF),
            pltpu.VMEM((2, HEADS, BLK), F32),
            pltpu.VMEM((2, WIDTH, BLK), BF),
            pltpu.VMEM((16, BLK, BLK), BF),
        ),
        in_specs=[hbm] * 4 + [vm] * 4,
        out_specs=(vm,) * 8,
        scratch_shapes=[
            pltpu.VMEM((32, ROWS, WIDTH), BF),
            *[pltpu.VMEM((WIDTH, WIDTH), BF)] * 6,
            pltpu.VMEM((4, 2, BLK, WIDTH), BF),
            pltpu.VMEM((8, 8, BLK), I32),
            pltpu.VMEM((8, 8, BLK), I32),
            dma((5, 6)), dma((5, 6)), dma((4, 4, 2)), dma((4, 4, 2)),
            dma((3, 2)), dma((3, 2)), dma((4, 2)), dma((4, 2)), dma((1,)), dma((1,)), dma((5,)),
        ],
        compiler_params=pltpu.CompilerParams(
            collective_id=0, has_side_effects=True, vmem_limit_bytes=44 << 20
        ),
        name="gather_project",
    )(*args)


def attention_kernel(
    qt, bits, self_score, self_value, kb, vt, et,
    acc_out, stat_out,
    lists, list_sem, rhs, acc, m, l, sched, sx, sy, mx, my,
):
    x, y, c, z = place()
    fetch = pltpu.make_async_copy(bits, lists, list_sem)
    fetch.start()

    def phase(g):
        return (4 * ((g // 2) * 8 + 2 * z + g % 2)) % 15

    def build(b, n):
        count = lists[b, 3, 0]

        def inner(t, n):
            first = lists[b, 1, 2 * t]
            live = 2 * t + 1 < count
            second = jnp.where(live, lists[b, 1, jnp.minimum(2 * t + 1, SLOTS - 1)], first)
            sched[0, n] = b
            sched[1, n] = first
            sched[2, n] = second
            sched[3, n] = phase(first)
            sched[4, n] = jnp.where(live, phase(second), 15)
            return n + 1

        return lax.fori_loop(0, (count + 1) // 2, inner, n)

    fetch.wait()
    steps = lax.fori_loop(0, 8, build, 0)
    for extra in range(2):
        for f in range(5):
            sched[f, steps + extra] = 15 if f >= 3 else 0
    even = 2 * ((steps + 1) // 2)

    def prepare(b, carry):
        brow = bits[b, 0:1, :]
        rr = lax.broadcasted_iota(I32, (32, BLK), 0)
        on = (jnp.broadcast_to(brow, (32, BLK)) >> rr) & 1
        g = jnp.where(on == 1, 0.0, OUT_MASK)
        g = jnp.where(rr < 30, g, jnp.where(rr == 31, OUT_MASK, 0.0)).astype(BF)
        gg = jnp.concatenate([g, g], 1)
        z64 = jnp.zeros((HD, BLK), BF)
        for p in range(4):
            rhs[b, p, 0:64, 0:128] = qt[b, 128 * p : 128 * p + 64, :]
            rhs[b, p, 0:64, 128:256] = z64
            rhs[b, p, 64:128, 0:128] = z64
            rhs[b, p, 64:128, 128:256] = qt[b, 128 * p + 64 : 128 * p + 128, :]
            rhs[b, p, 128:160, :] = gg
            rhs[b, p, 160:256, :] = jnp.zeros((96, 256), BF)
        m[b] = jnp.full((HEADS, BLK), FLOOR, F32)
        l[b] = jnp.zeros((HEADS, BLK), F32)
        acc[b] = jnp.zeros((WIDTH, BLK), F32)
        return carry

    lax.fori_loop(0, 8, prepare, 0)
    for cc in range(2):
        b = 2 * z + cc
        start = (dst_index(x, z - y + 4, cc) * 8 + 2 * z + flip(c, cc)) * BLK
        lanes = lax.broadcasted_iota(I32, (1, BLK), 1)
        on = (bits[b, 0:1, :] >> ((start + lanes) % 30)) & 1
        extra = jnp.broadcast_to(on, (HEADS, BLK)) == 0
        m[b] = jnp.where(extra, self_score[cc], FLOOR)
        l[b] = jnp.where(extra, 1.0, 0.0)
        acc[b] = jnp.where(
            jnp.broadcast_to(on, (WIDTH, BLK)) == 0, self_value[cc].astype(F32), 0.0
        )

    def scores(i, out, tops, p):
        e0, e1, b = et[sched[3, i]], et[sched[4, i]], sched[0, i]
        cols = slice(128 * p, 128 * p + 128)
        k0, k1 = kb[sched[1, i], :, cols], kb[sched[2, i], :, cols]
        lhs = jnp.concatenate([jnp.concatenate([k0, e0], 1), jnp.concatenate([k1, e1], 1)], 0)
        s = jnp.dot(lhs, rhs[b, p], preferred_element_type=F32)
        out[p] = s
        top = jnp.max(s.reshape(32, 8, 256), axis=0)
        tops[2 * p] = top[:, :128]
        tops[2 * p + 1] = top[:, 128:]

    def soften(i, cur, tops, h):
        b = sched[0, i]
        p, side = h // 2, h % 2
        old = m[b, h : h + 1, :]
        top = jnp.maximum(old, jnp.max(tops[h], axis=0, keepdims=True))
        factor = jnp.exp(old - top)
        w = jnp.exp(cur[p, :, 128 * side : 128 * side + 128] - top)
        m[b, h : h + 1, :] = top
        l[b, h : h + 1, :] = l[b, h : h + 1, :] * factor + jnp.sum(w, axis=0, keepdims=True)
        return w.astype(BF), factor

    def pair(i, cur, tops, p):
        b = sched[0, i]
        made = [soften(i, cur, tops, 2 * p + side) for side in range(2)]
        rows = slice(128 * p, 128 * p + 128)
        v = jnp.concatenate([vt[sched[1, i], rows, :], vt[sched[2, i], rows, :]], 1)
        o = jnp.dot(v, jnp.concatenate([w for w, _ in made], 1), preferred_element_type=F32)
        for side in range(2):
            rows = slice(128 * p + 64 * side, 128 * p + 64 * side + 64)
            block = o[64 * side : 64 * side + 64, 128 * side : 128 * side + 128]
            acc[b, rows, :] = acc[b, rows, :] * made[side][1] + block

    def step(i, cur, tops, nxt, next_tops):
        for p in range(4):
            scores(i + 1, nxt, next_tops, p)
            pair(i, cur, tops, p)

    for p in range(4):
        scores(0, sx, mx, p)

    def body(j, carry):
        step(2 * j, sx, mx, sy, my)
        step(2 * j + 1, sy, my, sx, mx)
        return carry

    lax.fori_loop(0, even // 2, body, 0)
    acc_out[...] = acc[...].astype(BF)
    stat_out[:, 0:8, :] = m[...]
    stat_out[:, 8:16, :] = l[...]


def attention_call(ints, qt, self_score, self_value, kb, vt, et):
    vm = pl.BlockSpec(memory_space=pltpu.VMEM)
    return pl.pallas_call(
        attention_kernel,
        out_shape=(
            pltpu.VMEM((8, WIDTH, BLK), BF),
            pltpu.VMEM((8, 16, BLK), F32),
        ),
        in_specs=[vm] * 7,
        out_specs=(vm, vm),
        scratch_shapes=[
            pltpu.SMEM((8, 8, BLK), I32),
            pltpu.SemaphoreType.DMA,
            pltpu.VMEM((8, 4, 256, 256), BF),
            pltpu.VMEM((8, WIDTH, BLK), F32),
            pltpu.VMEM((8, HEADS, BLK), F32),
            pltpu.VMEM((8, HEADS, BLK), F32),
            pltpu.SMEM((5, 136), I32),
            pltpu.VMEM((4, 256, 256), F32),
            pltpu.VMEM((4, 256, 256), F32),
            pltpu.VMEM((8, 8, BLK), F32),
            pltpu.VMEM((8, 8, BLK), F32),
        ],
        compiler_params=pltpu.CompilerParams(vmem_limit_bytes=24 << 20),
        name="block_attention",
    )(qt, ints, self_score, self_value, kb, vt, et)


def merge_kernel(
    acc, stat, dq, ids, w_out,
    updated_out, pooled_out,
    acc_got, stat_got, acc_way, stat_way, made, mine, part, ring_part, total, all_part,
    a_send, a_recv, s_send, s_recv, u_send, u_recv, r_send, r_recv, g_send, g_recv,
):
    x, y, c, z = place()
    me = dst_index(x, y, c)
    ring = []
    for dy in range(4):
        for dc in range(2):
            if dy or dc:
                ring.append((dy, dc, (dst_index(x, y + dy, flip(c, dc)), z)))
    far = []
    for dx in range(4):
        for dz in range(4):
            if dx or dz:
                far.append((dx, dz, (dst_index(x + dx, y, c), (z + dz) % 4)))
    barrier = pltpu.get_barrier_semaphore()
    for _, _, peer in ring + far:
        pl.semaphore_signal(barrier, inc=1, device_id=peer, device_id_type=MESH)
    pl.semaphore_wait(barrier, len(ring) + len(far))

    def remote(src, dst, send, recv, to):
        return pltpu.make_async_remote_copy(
            src_ref=src, dst_ref=dst, send_sem=send, recv_sem=recv, device_id=to, device_id_type=MESH
        )

    sent = []

    def go(copy):
        copy.start()
        sent.append(copy)

    zup, zdown, zfar = (z + 1) % 4, (z + 3) % 4, (z + 2) % 4

    def ship(slot, acc_ref, stat_ref, to):
        go(remote(acc_ref, acc_got.at[slot], a_send.at[slot], a_recv.at[slot], (me, to)))
        go(remote(stat_ref, stat_got.at[slot], s_send.at[slot], s_recv.at[slot], (me, to)))

    def landed(slot):
        remote(acc.at[0], acc_got.at[slot], a_send.at[slot], a_recv.at[slot], (me, zup)).wait_recv()
        remote(stat.at[0], stat_got.at[slot], s_send.at[slot], s_recv.at[slot], (me, zup)).wait_recv()

    for side, to in ((0, zup), (1, zdown)):
        ship(side, acc.at[2 * zfar + side], stat.at[2 * zfar + side], to)
    for side, to in ((0, zup), (1, zdown)):
        b = 2 * to + 1 - side
        ship(2 + side, acc.at[b], stat.at[b], to)

    def weigh(stats):
        top = stats[0][0:8]
        for s in stats[1:]:
            top = jnp.maximum(top, s[0:8])
        factors = [jnp.exp(s[0:8] - top) for s in stats]
        return top, factors, sum(f * s[8:16] for f, s in zip(factors, stats))

    for side, to in ((0, zup), (1, zdown)):
        b = 2 * to + side
        landed(side)
        top, factors, whole = weigh([stat[b], stat_got[side]])
        stat_way[side, 0:8] = top
        stat_way[side, 8:16] = whole
        for h in range(HEADS):
            rows = slice(64 * h, 64 * h + 64)
            acc_way[side, rows] = (
                acc[b, rows, :].astype(F32) * factors[0][h : h + 1, :]
                + acc_got[side, rows, :].astype(F32) * factors[1][h : h + 1, :]
            ).astype(BF)
        ship(4 + side, acc_way.at[side], stat_way.at[side], to)
    for side in range(2):
        landed(2 + side)
    yy = (z - y + 4) % 4
    for cc in range(2):
        b = 2 * z + cc
        landed(4 + cc)
        slots = (3 - cc, 4 + cc)
        _, factors, whole = weigh([stat[b]] + [stat_got[k] for k in slots])
        inv = 1.0 / whole
        factors = [f * inv for f in factors]
        pieces = []
        for h in range(HEADS):
            rows = slice(64 * h, 64 * h + 64)
            o = acc[b, rows, :].astype(F32) * factors[0][h : h + 1, :]
            for n, k in enumerate(slots):
                o = o + acc_got[k, rows, :].astype(F32) * factors[n + 1][h : h + 1, :]
            pieces.append(o)
        att = jnp.concatenate(pieces, 0).astype(BF).T
        mixed = jnp.dot(att, w_out[...], preferred_element_type=F32)
        new = (dq[cc].astype(F32) + mixed).astype(BF)
        made[cc] = new
        gid = ids[b, 2:3, :]
        graph = lax.broadcasted_iota(I32, (8, BLK), 0) % 4
        member = jnp.where(jnp.broadcast_to(gid, (8, BLK)) == graph, 1.0, 0.0)
        sums = jnp.dot(member.astype(BF), new, preferred_element_type=F32)
        low = lax.broadcasted_iota(I32, (8, 256), 0) < 4
        counts = jnp.broadcast_to(jnp.sum(member, axis=1, keepdims=True), (8, BLK))
        both = jnp.concatenate([jnp.where(low, sums[:, :256], sums[:, 256:]), counts], 1)
        part[...] = both if cc == 0 else part[...] + both
    for cc in range(2):
        own = jnp.logical_and(yy == y, c == cc)
        half = flip(c, cc)
        copy = remote(made.at[cc], mine.at[half], u_send.at[cc], u_recv.at[half], (dst_index(x, yy, cc), z))
        local = pltpu.make_async_copy(made.at[cc], mine.at[half], u_recv.at[half])
        pl.when(jnp.logical_not(own))(copy.start)
        pl.when(own)(local.start)
    for dy, dc, to in ring:
        k = 2 * dy + dc
        go(remote(part, ring_part.at[k], r_send.at[k], r_recv.at[k], to))
    whole = part[...]
    for dy, dc, to in ring:
        k = 2 * dy + dc
        remote(part, ring_part.at[k], r_send.at[k], r_recv.at[k], to).wait_recv()
        whole = whole + ring_part[k]
    total[...] = whole
    for dx, dz, to in far:
        k = 4 * dx + dz
        go(remote(total, all_part.at[k], g_send.at[k], g_recv.at[k], to))
    for half in range(2):
        pltpu.make_async_copy(made.at[half], mine.at[half], u_recv.at[half]).wait()
    updated_out[0:BLK, :] = mine[0]
    updated_out[BLK:ROWS, :] = mine[1]
    for dx, dz, to in far:
        k = 4 * dx + dz
        remote(total, all_part.at[k], g_send.at[k], g_recv.at[k], to).wait_recv()
        whole = whole + all_part[k]
    scale = 1.0 / jnp.sqrt(jnp.concatenate([whole[0:4, 256:]] * 2, 1))
    pooled_out[:, 0:256] = whole[0:4, 0:256] * scale
    pooled_out[:, 256:512] = whole[4:8, 0:256] * scale
    for cc in range(2):
        own = jnp.logical_and(yy == y, c == cc)
        copy = remote(
            made.at[cc], mine.at[flip(c, cc)], u_send.at[cc], u_recv.at[flip(c, cc)],
            (dst_index(x, yy, cc), z),
        )
        pl.when(jnp.logical_not(own))(copy.wait_send)
    for copy in sent:
        copy.wait_send()


def merge_call(acc, stat, dq, ids, w_out):
    vm = pl.BlockSpec(memory_space=pltpu.VMEM)
    dma = pltpu.SemaphoreType.DMA
    return pl.pallas_call(
        merge_kernel,
        out_shape=(
            jax.ShapeDtypeStruct((ROWS, WIDTH), BF),
            jax.ShapeDtypeStruct((4, WIDTH), F32),
        ),
        in_specs=[vm] * 5,
        out_specs=(vm, vm),
        scratch_shapes=[
            pltpu.VMEM((6, WIDTH, BLK), BF),
            pltpu.VMEM((6, 16, BLK), F32),
            pltpu.VMEM((2, WIDTH, BLK), BF),
            pltpu.VMEM((2, 16, BLK), F32),
            pltpu.VMEM((2, BLK, WIDTH), BF),
            pltpu.VMEM((2, BLK, WIDTH), BF),
            pltpu.VMEM((8, 256 + BLK), F32),
            pltpu.VMEM((8, 8, 256 + BLK), F32),
            pltpu.VMEM((8, 256 + BLK), F32),
            pltpu.VMEM((16, 8, 256 + BLK), F32),
            dma((6,)), dma((6,)), dma((6,)), dma((6,)), dma((2,)), dma((2,)),
            dma((8,)), dma((8,)), dma((16,)), dma((16,)),
        ],
        compiler_params=pltpu.CompilerParams(
            collective_id=1, has_side_effects=True, vmem_limit_bytes=16 << 20
        ),
        name="merge_project_pool",
    )(acc, stat, dq, ids, w_out)


def shards(features, w_query, w_key, w_value, w_out, node_bits, block_src, block_count, graph_ids):
    kb, vt, qt, got, dq, self_score, self_value, et = gather_call(
        features, w_query, w_key, w_value,
        node_bits.reshape(8, BLK), block_src, block_count.reshape(1, 8), graph_ids.reshape(2, BLK),
    )
    acc, stat = attention_call(
        got, qt, self_score, self_value, kb.reshape(64, BLK, WIDTH), vt.reshape(64, WIDTH, BLK), et
    )
    return merge_call(acc, stat, dq, got, w_out)


def solution(mesh):
    placed = (
        P(("dst", "src"), None),
        P(),
        P(),
        P(),
        P(),
        P("dst"),
        P("dst", "src", None),
        P("dst", "src"),
        P(("dst", "src")),
    )
    return jax.shard_map(
        shards,
        mesh=mesh,
        in_specs=placed,
        out_specs=(P(("dst", "src"), None), P()),
        check_vma=False,
    )
```
